32 devices in a mesh: ctx: 4 (over x, core), head: 4 (over z), seq: 2 (over y).
Axes of the slice: x: 2, y: 2, z: 4, core: 2. Of those that a mesh axis runs over, the one named last changes fastest.
Arguments:
- attn_query: bfloat16 [4096, 5120], P(('seq', 'ctx'), 'head'), parts along dimension 0, may hold values from -7.5 to 7.5
- attn_key: bfloat16 [4096, 5120], P(('seq', 'ctx'), 'head'), parts along dimension 0, may hold values from -7.5 to 7.5
- attn_value: bfloat16 [4096, 5120], P(('seq', 'ctx'), 'head'), parts along dimension 0, may hold values from -6 to 6
- fw_query: bfloat16 [4096, 5120], P(('seq', 'ctx'), 'head'), parts along dimension 0, may hold values from -6 to 6
- fw_key: bfloat16 [4096, 5120], P(('seq', 'ctx'), 'head'), parts along dimension 0, may hold values from -6 to 6
- fw_value: bfloat16 [4096, 5120], P(('seq', 'ctx'), 'head'), parts along dimension 0, may hold values from -6 to 6
- fw_rate: float32 [4096, 8], P(('seq', 'ctx'), 'head'), parts along dimension 0, may hold values from 0.005 to 0.05
- fast_weights: float32 [1280, 15360], P(('seq', 'ctx'), 'head'), parts along dimension 0, may hold values from -50 to 50
- momentum: float32 [1280, 15360], P(('seq', 'ctx'), 'head'), parts along dimension 0, may hold values from -6 to 6
Outputs:
- attn_out: bfloat16 [4096, 5120], P(('seq', 'ctx'), 'head'), parts along dimension 0
- fw_out: bfloat16 [4096, 5120], P(('seq', 'ctx'), 'head'), parts along dimension 0
- new_weights: float32 [1280, 15360], P(('seq', 'ctx'), 'head'), parts along dimension 0
- new_momentum: float32 [1280, 15360], P(('seq', 'ctx'), 'head'), parts along dimension 0
The draws below stay inside these ranges and needn't reach their ends.
There are 2 independent parts, one for each index of `seq`. The reference program is written for one: setup_inputs(seed, part) draws one part's arguments, and reference() takes and returns one part's arrays. A program takes and returns all parts, laid end to end along the dimension named above; each array names one. Nothing has to cross between parts.
All inputs are finite; a program needn't handle non-finite values.
Results may differ from the reference program's by a relative error of at most 0.014.
Values may be sent and summed in bfloat16 or wider, within the bound.
No kernel may reach another device: no remote copies, remote signals or barrier semaphores. Data moves between devices by JAX's collectives and lax.ppermute only.
A program may use at most 128 MiB of HBM per device.

```python
import math
import jax
import jax.numpy as jnp
from jax import lax

AHEADS = 40
HD = 128
FHEADS = 8
FD = 640
WINDOW = 1024
TOKENS = 2048


def attention_pair(key):
    query_key, keys_key = jax.random.split(jax.random.fold_in(key, 11), 2)
    shape_all = (TOKENS, AHEADS * HD)
    queries = 1.5 * jax.random.truncated_normal(query_key, -5.0, 5.0, shape_all, jnp.float32)
    key_rows = 1.5 * jax.random.truncated_normal(keys_key, -5.0, 5.0, shape_all, jnp.float32)
    return (queries, key_rows)


def draw_attn_query(key, part):
    return attention_pair(key)[0].astype(jnp.bfloat16)


def draw_attn_key(key, part):
    return attention_pair(key)[1].astype(jnp.bfloat16)


def draw_fast_weights(key, part):
    base_key = jax.random.fold_in(jax.random.fold_in(key, 23), 0)
    width_all = FHEADS * 3 * FD
    entries = jax.random.truncated_normal(base_key, -5.0, 5.0, (FD, width_all), jnp.float32)
    return entries


def block_levels(key, dims, cuts, least, high):
    def one(dim, blocks):
        heights = jax.random.uniform(jax.random.fold_in(jax.random.fold_in(key, 6), dim), (blocks,), jnp.float32, least / len(cuts), high / len(cuts))
        return jnp.repeat(jnp.exp(heights), dims[dim] // blocks).reshape((-1,) + (1,) * (len(dims) - dim - 1))

    gain = one(*cuts[0])
    for cut in cuts[1:]:
        gain = gain * one(*cut)
    return gain


def bell_draw(stream_key, shape, width, reach, pieces=(), kind=jnp.bfloat16):
    level = block_levels(stream_key, shape, pieces, -0.22, 0.18) if pieces else 1.0
    values = jax.random.normal(stream_key, shape, jnp.float32) * width * level
    return jnp.minimum(jnp.maximum(values, -reach), reach).astype(kind)


def setup_inputs(seed: int = 0, part: int = 0) -> dict:
    key_of = jax.random.split(jax.random.key(seed), 10)
    part_keys = jax.random.split(jax.random.fold_in(key_of[9], part), 10)
    attn_query = draw_attn_query(jax.random.fold_in(jax.random.fold_in(key_of[9], part), 71), part)
    attn_key = draw_attn_key(jax.random.fold_in(jax.random.fold_in(key_of[9], part), 71), part)
    attn_value = bell_draw(part_keys[2], (TOKENS, AHEADS * HD), 1.0, 6.0, ((0, 4), (1, 4)))
    fw_query = bell_draw(part_keys[3], (TOKENS, FHEADS * FD), 1.0, 6.0, ((0, 4), (1, 4)))
    fw_key = bell_draw(part_keys[4], (TOKENS, FHEADS * FD), 1.0, 6.0, ((0, 4), (1, 4)))
    fw_value = bell_draw(part_keys[5], (TOKENS, FHEADS * FD), 1.0, 6.0, ((0, 4), (1, 4)))
    fw_rate = jnp.clip(jnp.exp(math.log(0.05) - 2.3025851 * jax.random.uniform(part_keys[6], (TOKENS, FHEADS), jnp.float32) ** block_levels(part_keys[6], (TOKENS, FHEADS), ((0, 4), (1, 4)), -0.2, 0.2)), 0.005, 0.05)
    fast_weights = draw_fast_weights(jax.random.fold_in(jax.random.fold_in(key_of[9], part), 71), part)
    momentum = bell_draw(part_keys[8], (FD, FHEADS * 3 * FD), 0.5, 6.0, ((0, 4), (1, 4)), jnp.float32)
    return {"attn_query": attn_query, "attn_key": attn_key, "attn_value": attn_value, "fw_query": fw_query, "fw_key": fw_key, "fw_value": fw_value, "fw_rate": fw_rate, "fast_weights": fast_weights, "momentum": momentum}


EPSILON = 1e-06
DECAY = 0.9

def window_attention(attn_query, attn_key, attn_value):
    head_count = attn_query.shape[1] // HD
    block_rows = min(512, TOKENS)
    query_all = attn_query.reshape(TOKENS, head_count, HD)
    padding = jnp.zeros((WINDOW, head_count, HD), attn_key.dtype)
    key_all = jnp.concatenate([padding, attn_key.reshape(TOKENS, head_count, HD)], axis=0)
    value_all = jnp.concatenate([padding, attn_value.reshape(TOKENS, head_count, HD)], axis=0)
    score_scale = HD ** (-0.5)

    def one_block(begin_row):
        query_block = lax.dynamic_slice_in_dim(query_all, begin_row, block_rows, 0)
        key_block = lax.dynamic_slice_in_dim(key_all, begin_row, WINDOW + block_rows, 0)
        value_block = lax.dynamic_slice_in_dim(value_all, begin_row, WINDOW + block_rows, 0)
        scores = jnp.einsum('qhd,khd->hqk', query_block.astype(jnp.float32), key_block.astype(jnp.float32)) * score_scale
        row_index = jnp.arange(block_rows, dtype=jnp.int32)[:, None]
        key_index = jnp.arange(WINDOW + block_rows, dtype=jnp.int32)[None, :]
        allowed = (key_index > row_index) & (key_index <= row_index + WINDOW) & (begin_row - WINDOW + key_index >= 0)
        scores = jnp.where(allowed[None], scores, -jnp.inf)
        highest = lax.optimization_barrier(jnp.max(scores, axis=2, keepdims=True))
        exponent = jnp.exp(scores - highest)
        denominator = lax.optimization_barrier(jnp.sum(exponent, axis=2))
        prob_low = exponent.astype(jnp.bfloat16)
        mixed = jnp.einsum('hqk,khd->qhd', prob_low.astype(jnp.float32), value_block.astype(jnp.float32))
        return (mixed / jnp.transpose(denominator)[:, :, None]).astype(jnp.bfloat16)
    block_starts = jnp.arange(TOKENS // block_rows, dtype=jnp.int32) * block_rows
    block_outs = lax.map(one_block, block_starts)
    return block_outs.reshape(TOKENS, head_count * HD)

def local_grads(gate_pre, up_pre, back_hidden):
    sigmoid_gate = jax.nn.sigmoid(gate_pre)
    gate_silu = gate_pre * sigmoid_gate
    hidden = (gate_silu * up_pre).astype(jnp.bfloat16)
    gate_grad = (back_hidden * up_pre * sigmoid_gate * (1.0 + gate_pre * (1.0 - sigmoid_gate))).astype(jnp.bfloat16)
    up_grad = (back_hidden * gate_silu).astype(jnp.bfloat16)
    return (hidden, gate_grad, up_grad)

def renormalize(weights, moved):
    shape_split = (weights.shape[0], -1, FD)
    before_sq = lax.optimization_barrier(jnp.mean(jnp.square(weights.reshape(shape_split)), axis=2, keepdims=True))
    after_sq = lax.optimization_barrier(jnp.mean(jnp.square(moved.reshape(shape_split)), axis=2, keepdims=True))
    factor = jnp.sqrt(before_sq + EPSILON) * lax.rsqrt(after_sq + EPSILON)
    return (moved.reshape(shape_split) * factor).reshape(moved.shape)

def apply_query(weights_low, queries):
    inv_root = FD ** (-0.5)
    query_gate = jnp.dot(queries, weights_low[:, :FD].T, preferred_element_type=jnp.float32) * inv_root
    query_up = jnp.dot(queries, weights_low[:, FD:2 * FD].T, preferred_element_type=jnp.float32) * inv_root
    query_hidden = (query_gate * jax.nn.sigmoid(query_gate) * query_up).astype(jnp.bfloat16)
    result = jnp.dot(query_hidden, weights_low[:, 2 * FD:].T, preferred_element_type=jnp.float32) * inv_root
    return result.astype(jnp.bfloat16)

def fast_head(weights, moment, key_rows, values, queries, rate_column):
    inv_root = FD ** (-0.5)
    weights_low = weights.astype(jnp.bfloat16)
    gate_pre = jnp.dot(key_rows, weights_low[:, :FD].T, preferred_element_type=jnp.float32) * inv_root
    up_pre = jnp.dot(key_rows, weights_low[:, FD:2 * FD].T, preferred_element_type=jnp.float32) * inv_root
    scaled = (rate_column[:, None] * values.astype(jnp.float32)).astype(jnp.bfloat16)
    back_hidden = jnp.dot(scaled, weights_low[:, 2 * FD:], preferred_element_type=jnp.float32) * inv_root
    hidden, gate_grad, up_grad = local_grads(gate_pre, up_pre, back_hidden)
    update = jnp.concatenate([jnp.dot(gate_grad.T, key_rows, preferred_element_type=jnp.float32), jnp.dot(up_grad.T, key_rows, preferred_element_type=jnp.float32), jnp.dot(scaled.T, hidden, preferred_element_type=jnp.float32)], axis=1)
    moment_next = DECAY * moment + update
    weights_next = renormalize(weights, weights + moment_next)
    return (apply_query(weights_next.astype(jnp.bfloat16), queries), weights_next, moment_next)

def reference(attn_query, attn_key, attn_value, fw_query, fw_key, fw_value, fw_rate, fast_weights, momentum):
    attn_out = window_attention(attn_query, attn_key, attn_value)
    outputs = []
    weights_list = []
    moment_list = []
    span = 3 * FD
    for head_index in range(FHEADS):
        result, weights_next, moment_next = fast_head(fast_weights[:, head_index * span:(head_index + 1) * span], momentum[:, head_index * span:(head_index + 1) * span], fw_key[:, head_index * FD:(head_index + 1) * FD], fw_value[:, head_index * FD:(head_index + 1) * FD], fw_query[:, head_index * FD:(head_index + 1) * FD], fw_rate[:, head_index])
        outputs.append(result)
        weights_list.append(weights_next)
        moment_list.append(moment_next)
    fw_out = jnp.concatenate(outputs, axis=1)
    new_weights = jnp.concatenate(weights_list, axis=1)
    new_momentum = jnp.concatenate(moment_list, axis=1)
    return (attn_out, fw_out, new_weights, new_momentum)
```

```python
import functools
import math

import jax
import jax.numpy as jnp
from jax import lax
from jax.experimental import pallas as pl
from jax.experimental.pallas import tpu as pltpu
from jax.sharding import PartitionSpec as P

HD = 128
FD = 640
WINDOW = 1024
EPSILON = 1e-06
DECAY = 0.9
SPAN = 3 * FD
INV_ROOT = FD ** (-0.5)
EXP2_SCALE = HD ** (-0.5) * math.log2(math.e)
LOWEST = -1e30
F32 = jnp.float32
BF16 = jnp.bfloat16
ANY = pl.BlockSpec(memory_space=pl.ANY)


def dot(a, b, a_dim, b_dim):
    return lax.dot_general(a, b, (((a_dim,), (b_dim,)), ((), ())), preferred_element_type=F32)


def cost(flops, bytes_accessed, transcendentals=0):
    return pl.CostEstimate(
        flops=int(flops), bytes_accessed=int(bytes_accessed), transcendentals=int(transcendentals)
    )


def attention_kernel(shape_kind, has_state, last, offset, *refs):
    if has_state:
        q_ref, k_ref, v_ref, o_in_ref, st_in_ref = refs[:5]
        outs = refs[5:]
    else:
        q_ref, k_ref, v_ref = refs[:3]
        outs = refs[3:]
    head = pl.program_id(0)
    heads = pl.num_programs(0)
    scores = dot(k_ref[...], q_ref[...], 1, 1)
    if shape_kind != "full":
        key_row = lax.broadcasted_iota(jnp.int32, scores.shape, 0)
        query_row = lax.broadcasted_iota(jnp.int32, scores.shape, 1)
        allowed = key_row <= query_row if shape_kind == "causal" else key_row > query_row
        scores = jnp.where(allowed, scores, LOWEST)
    highest = jnp.max(scores, axis=0, keepdims=True)
    if has_state:
        valid = lax.axis_index("ctx") >= offset
        before = jnp.where(valid, st_in_ref[pl.ds(head, 1), :], LOWEST)
        highest = jnp.maximum(highest, before)
    weights = jnp.exp2((scores - highest) * EXP2_SCALE)
    total = jnp.sum(weights, axis=0, keepdims=True)
    mixed = dot(v_ref[...], weights.astype(BF16), 0, 0)
    if has_state:
        keep = jnp.exp2((before - highest) * EXP2_SCALE)
        total = total + keep * st_in_ref[pl.ds(heads + head, 1), :]
        mixed = mixed + keep * o_in_ref[...].astype(F32)
    if last:
        outs[0][...] = (mixed / total).T.astype(BF16)
    else:
        outs[0][...] = mixed.astype(BF16)
        outs[1][pl.ds(head, 1), :] = highest
        outs[1][pl.ds(heads + head, 1), :] = total


def attention_step(shape_kind, queries, keys, values, state, last, offset):
    rows, width = queries.shape
    heads = width // HD
    column = pl.BlockSpec((rows, HD), lambda h: (0, h))
    turned = pl.BlockSpec((HD, rows), lambda h: (h, 0))
    stats = pl.BlockSpec((2 * heads, rows), lambda h: (0, 0))
    in_specs = [column, column, column]
    args = [queries, keys, values]
    if state is not None:
        in_specs += [turned, stats]
        args += list(state)
    if last:
        out_shape = jax.ShapeDtypeStruct((rows, width), BF16)
        out_specs = column
    else:
        out_shape = (
            jax.ShapeDtypeStruct((width, rows), BF16),
            jax.ShapeDtypeStruct((2 * heads, rows), F32),
        )
        out_specs = (turned, stats)
    return pl.pallas_call(
        functools.partial(attention_kernel, shape_kind, state is not None, last, offset),
        grid=(heads,),
        in_specs=in_specs,
        out_specs=out_specs,
        out_shape=out_shape,
        cost_estimate=cost(4 * rows * rows * width, 5 * rows * width * 2, rows * rows * heads),
        name="attend_" + shape_kind,
    )(*args)


def shifted(arrays, by, low, high):
    pairs = [(i, i + by) for i in range(low, high)]
    return [lax.ppermute(array, "ctx", pairs) for array in arrays]


def fetch_rows(parts, masks, target, sems):
    index = lax.axis_index("ctx")
    copies = []
    for number, (part, mask) in enumerate(zip(parts, masks)):
        rows = part.shape[0]
        if mask is None:
            place = target
        else:
            place = target.at[pl.ds(pl.multiple_of((index ^ mask) * rows, 32), rows)]
        copy = pltpu.make_async_copy(part, place, sems.at[number])
        copy.start()
        copies.append(copy)
    return copies


def grads_kernel(masks, split, head, *refs):
    count = len(masks)
    key_ref, value_ref, rate_ref = refs[:3]
    parts = refs[3 : 3 + count]
    outs = refs[3 + count : -7]
    low, scaled, hidden, gate_grad, up_grad, update, sems = refs[-7:]
    copies = fetch_rows(parts, masks, low, sems)
    rate = rate_ref[:, head : head + 1]
    scaled[...] = (rate * value_ref[...].astype(F32)).astype(BF16)
    for copy in copies:
        copy.wait()
    tokens = key_ref.shape[0]
    block = min(256, tokens)

    def forward(step, carry):
        rows = pl.ds(pl.multiple_of(step * block, block), block)
        keys = key_ref[rows, :]
        gate = dot(keys, low[:, :FD], 1, 1) * INV_ROOT
        up = dot(keys, low[:, FD : 2 * FD], 1, 1) * INV_ROOT
        back = dot(scaled[rows, :], low[:, 2 * FD :], 1, 0) * INV_ROOT
        sigmoid = 1.0 / (1.0 + jnp.exp(-gate))
        silu = gate * sigmoid
        hidden[rows, :] = (silu * up).astype(BF16)
        gate_grad[rows, :] = (back * up * sigmoid * (1.0 + gate * (1.0 - sigmoid))).astype(BF16)
        up_grad[rows, :] = (back * silu).astype(BF16)
        return carry

    lax.fori_loop(0, tokens // block, forward, 0)

    def backward(step, carry):
        rows = pl.ds(pl.multiple_of(step * 128, 128), 128)
        update[rows, :FD] = dot(gate_grad[:, rows], key_ref[...], 0, 0)
        update[rows, FD : 2 * FD] = dot(up_grad[:, rows], key_ref[...], 0, 0)
        update[rows, 2 * FD :] = dot(scaled[:, rows], hidden[...], 0, 0)
        return carry

    lax.fori_loop(0, FD // 128, backward, 0)
    if split:
        index = lax.axis_index("ctx")
        for out, mask in zip(outs, (3, 1, 2, 0)):
            rows = out.shape[0]
            out[...] = update[pl.ds(pl.multiple_of((index ^ mask) * rows, 32), rows), :].astype(out.dtype)
    else:
        outs[0][...] = update[...]


def head_grads(fw_key, fw_value, fw_rate, gathered, head, split):
    tokens = fw_key.shape[0]
    parts = [part for part, _ in gathered]
    masks = [mask for _, mask in gathered]
    column = pl.BlockSpec((tokens, FD), lambda i: (0, head))
    if split:
        rows = parts[0].shape[0]
        out_shape = tuple(jax.ShapeDtypeStruct((rows, SPAN), kind) for kind in (BF16, BF16, F32, F32))
    else:
        out_shape = (jax.ShapeDtypeStruct((FD, SPAN), F32),)
    out_specs = tuple(pl.BlockSpec(out.shape, lambda i: (0, 0)) for out in out_shape)
    return pl.pallas_call(
        functools.partial(grads_kernel, masks, split, head),
        grid=(1,),
        in_specs=[column, column, pl.BlockSpec(fw_rate.shape, lambda i: (0, 0))] + [ANY] * len(parts),
        out_specs=out_specs,
        out_shape=out_shape,
        scratch_shapes=[
            pltpu.VMEM((FD, SPAN), BF16),
            pltpu.VMEM((tokens, FD), BF16),
            pltpu.VMEM((tokens, FD), BF16),
            pltpu.VMEM((tokens, FD), BF16),
            pltpu.VMEM((tokens, FD), BF16),
            pltpu.VMEM((FD, SPAN), F32),
            pltpu.SemaphoreType.DMA((len(parts),)),
        ],
        cost_estimate=cost(12 * tokens * FD * FD, 8e6, tokens * FD),
        name="head_grads",
    )(fw_key, fw_value, fw_rate, *parts)


def move_kernel(sums, aliased, w_ref, m_ref, *refs):
    addends = refs[:sums]
    nw_ref, nm_ref, low_ref = refs[-3:]
    update = addends[0][...]
    for addend in addends[1:]:
        update = update + addend[...].astype(F32)
    weights = w_ref[...]
    momentum = DECAY * m_ref[...] + update
    moved = weights + momentum
    nm_ref[...] = momentum
    for part in range(3):
        cols = slice(part * FD, (part + 1) * FD)
        before = jnp.mean(jnp.square(weights[:, cols]), axis=1, keepdims=True)
        after = jnp.mean(jnp.square(moved[:, cols]), axis=1, keepdims=True)
        fresh = moved[:, cols] * (jnp.sqrt(before + EPSILON) * lax.rsqrt(after + EPSILON))
        nw_ref[:, cols] = fresh
        low_ref[:, cols] = fresh.astype(BF16)


def move_weights(fast_weights, momentum, addends, head, previous):
    rows = fast_weights.shape[0]
    block = 32 if rows % 32 == 0 else rows
    wide = pl.BlockSpec((block, SPAN), lambda i: (i, head))
    own = pl.BlockSpec((block, SPAN), lambda i: (i, 0))
    in_specs = [wide, wide] + [own] * len(addends)
    args = [fast_weights, momentum] + list(addends)
    aliases = {}
    if previous is not None:
        aliases = {len(args): 0, len(args) + 1: 1}
        in_specs += [ANY, ANY]
        args += list(previous)
    full = jax.ShapeDtypeStruct(fast_weights.shape, F32)
    return pl.pallas_call(
        functools.partial(move_kernel, len(addends), previous is not None),
        grid=(rows // block,),
        in_specs=in_specs,
        out_specs=(wide, wide, own),
        out_shape=(full, full, jax.ShapeDtypeStruct((rows, SPAN), BF16)),
        input_output_aliases=aliases,
        cost_estimate=cost(20 * rows * SPAN, 26 * rows * SPAN),
        name="move_weights",
    )(*args)


def query_kernel(masks, aliased, q_ref, *refs):
    count = len(masks)
    parts = refs[:count]
    out_ref, low, sems = refs[-3:]
    for copy in fetch_rows(parts, masks, low, sems):
        copy.wait()
    tokens = q_ref.shape[0]
    block = min(256, tokens)

    def one(step, carry):
        rows = pl.ds(pl.multiple_of(step * block, block), block)
        queries = q_ref[rows, :]
        gate = dot(queries, low[:, :FD], 1, 1) * INV_ROOT
        up = dot(queries, low[:, FD : 2 * FD], 1, 1) * INV_ROOT
        hidden = (gate * (1.0 / (1.0 + jnp.exp(-gate))) * up).astype(BF16)
        out_ref[rows, :] = (dot(hidden, low[:, 2 * FD :], 1, 1) * INV_ROOT).astype(BF16)
        return carry

    lax.fori_loop(0, tokens // block, one, 0)


def head_query(fw_query, gathered, head, previous):
    tokens = fw_query.shape[0]
    parts = [part for part, _ in gathered]
    masks = [mask for _, mask in gathered]
    column = pl.BlockSpec((tokens, FD), lambda i: (0, head))
    in_specs = [column] + [ANY] * len(parts)
    args = [fw_query] + parts
    aliases = {}
    if previous is not None:
        aliases = {len(args): 0}
        in_specs.append(ANY)
        args.append(previous)
    return pl.pallas_call(
        functools.partial(query_kernel, masks, previous is not None),
        grid=(1,),
        in_specs=in_specs,
        out_specs=column,
        out_shape=jax.ShapeDtypeStruct(fw_query.shape, BF16),
        scratch_shapes=[pltpu.VMEM((FD, SPAN), BF16), pltpu.SemaphoreType.DMA((len(parts),))],
        input_output_aliases=aliases,
        cost_estimate=cost(6 * tokens * FD * FD, 4e6, tokens * FD),
        name="head_query",
    )(*args)


def swapped(array, mask):
    devices = lax.axis_size("ctx")
    return lax.ppermute(array, "ctx", [(i, i ^ mask) for i in range(devices)])


def gather_rows(shard, paired):
    if not paired:
        return [(lax.all_gather(shard, "ctx", axis=0, tiled=True), None)]
    across = swapped(shard, 2)
    beside = swapped(shard, 1)
    return [(shard, 0), (beside, 1), (across, 2), (swapped(across, 1), 3)]


def sum_rows(pieces, paired):
    if not paired:
        return [lax.psum_scatter(pieces[0], "ctx", scatter_dimension=0, tiled=True)]
    far, near, across, own = pieces
    far = swapped(far, 1)
    near = swapped(near, 1)
    total = (across + far.astype(F32)).astype(BF16)
    return [own, near, swapped(total, 2)]


def per_device(
    attn_query, attn_key, attn_value, fw_query, fw_key, fw_value, fw_rate, fast_weights, momentum
):
    devices = lax.axis_size("ctx")
    rows = attn_query.shape[0]
    reach = WINDOW // rows
    head_local = fw_rate.shape[1]
    paired = devices == 4

    lows = [
        fast_weights[:, head * SPAN : (head + 1) * SPAN].astype(BF16) for head in range(head_local)
    ]
    gathered = [gather_rows(low, paired) for low in lows]

    travelling = [attn_query]
    for step in range(1, reach + 1):
        travelling.append(shifted([travelling[-1]], -1, 1, devices - step + 1)[0])

    pieces = [
        head_grads(fw_key, fw_value, fw_rate, gathered[head], head, paired)
        for head in range(head_local)
    ]
    sums = [sum_rows(piece, paired) for piece in pieces]

    state = None
    for step in range(reach, -1, -1):
        shape_kind = "causal" if step == 0 else "before" if step == reach else "full"
        state = attention_step(
            shape_kind, travelling[step], attn_key, attn_value, state, step == 0, 1
        )
        if step > 0:
            state = shifted(state, 1, 0, devices - step)
    attn_out = state

    new = None
    new_lows = []
    for head in range(head_local):
        new_weights, new_momentum, low = move_weights(
            fast_weights, momentum, sums[head], head, new
        )
        new = (new_weights, new_momentum)
        new_lows.append(low)
    new_gathered = [gather_rows(low, paired) for low in new_lows]
    fw_out = None
    for head in range(head_local):
        fw_out = head_query(fw_query, new_gathered[head], head, fw_out)
    return (attn_out, fw_out, new_weights, new_momentum)


def solution(mesh):
    spec = P(("seq", "ctx"), "head")
    return jax.shard_map(
        per_device, mesh=mesh, in_specs=(spec,) * 9, out_specs=(spec,) * 4, check_vma=False
    )
```

```python
import functools
import math

import jax
import jax.numpy as jnp
from jax import lax
from jax.experimental import pallas as pl
from jax.experimental.pallas import tpu as pltpu
from jax.sharding import PartitionSpec as P


HD = 128
FD = 640
EPSILON = 1e-06
DECAY = 0.9
SPAN = 3 * FD
INV_ROOT = FD ** (-0.5)
EXP2_SCALE = HD ** (-0.5) * math.log2(math.e)
LOWEST = -1e30
F32 = jnp.float32
BF16 = jnp.bfloat16
ANY = pl.BlockSpec(memory_space=pl.ANY)


def dot(a, b, a_dim, b_dim):
    return lax.dot_general(a, b, (((a_dim,), (b_dim,)), ((), ())), preferred_element_type=F32)


def cost(flops, bytes_accessed, transcendentals=0):
    return pl.CostEstimate(
        flops=int(flops), bytes_accessed=int(bytes_accessed), transcendentals=int(transcendentals)
    )


CHUNK = 128


def soft(scores, values):
    highest = jnp.max(scores, axis=0, keepdims=True)
    weights = jnp.exp2((scores - highest) * EXP2_SCALE)
    total = jnp.sum(weights, axis=0, keepdims=True)
    return dot(values, weights.astype(BF16), 0, 0), highest, total


def masked(scores, causal, first_key, first_query):
    key_row = lax.broadcasted_iota(jnp.int32, scores.shape, 0) + first_key
    query_row = lax.broadcasted_iota(jnp.int32, scores.shape, 1) + first_query
    allowed = key_row <= query_row if causal else key_row > query_row
    return jnp.where(allowed, scores, LOWEST)


def scaled_to(before, after):
    return jnp.exp2((before - after) * EXP2_SCALE)


def own_kernel(per_step, q_ref, k_ref, v_ref, o_ref, st_ref):
    for g in range(per_step):
        cols = slice(g * HD, (g + 1) * HD)
        for first in range(0, q_ref.shape[0], CHUNK):
            rows = slice(first, first + CHUNK)
            upto = first + CHUNK
            scores = masked(dot(k_ref[:upto, cols], q_ref[rows, cols], 1, 1), True, 0, first)
            mixed, highest, total = soft(scores, v_ref[:upto, cols])
            o_ref[cols, rows] = mixed.astype(BF16)
            st_ref[g : g + 1, rows] = highest
            st_ref[8 + g : 9 + g, rows] = total


def group_kernel(
    per_step, q_ref, far_ref, k_ref, v_ref, pk_ref, pv_ref, o_ref, st_ref, fo_ref, fst_ref, lo_ref, lst_ref
):
    leading = lax.axis_index("ctx") % 2 == 0
    for g in range(per_step):
        cols = slice(g * HD, (g + 1) * HD)
        top, bottom = slice(g, g + 1), slice(8 + g, 9 + g)
        for first in range(0, q_ref.shape[0], CHUNK):
            rows = slice(first, first + CHUNK)
            far = far_ref[rows, cols]
            scores = masked(dot(k_ref[first:, cols], far, 1, 1), False, first, first)
            far_o, far_m, far_l = soft(scores, v_ref[first:, cols])
            guest = jnp.where(leading, far, q_ref[rows, cols])
            mixed, highest, total = soft(dot(pk_ref[:, cols], guest, 1, 1), pv_ref[:, cols])
            far_top = jnp.where(leading, jnp.maximum(far_m, highest), far_m)
            far_keep = scaled_to(far_m, far_top)
            far_add = jnp.where(leading, scaled_to(highest, far_top), 0.0)
            fo_ref[cols, rows] = (far_o * far_keep + mixed * far_add).astype(BF16)
            fst_ref[top, rows] = far_top
            fst_ref[bottom, rows] = far_l * far_keep + total * far_add
            own_m = st_ref[top, rows]
            own_top = jnp.where(leading, own_m, jnp.maximum(own_m, highest))
            own_keep = scaled_to(own_m, own_top)
            own_add = jnp.where(leading, 0.0, scaled_to(highest, own_top))
            lo_ref[cols, rows] = (o_ref[cols, rows].astype(F32) * own_keep + mixed * own_add).astype(BF16)
            lst_ref[top, rows] = own_top
            lst_ref[bottom, rows] = st_ref[bottom, rows] * own_keep + total * own_add


def merge_kernel(per_step, o_ref, st_ref, fo_ref, fst_ref, out_ref):
    valid = lax.axis_index("ctx") >= 2
    for g in range(per_step):
        cols = slice(g * HD, (g + 1) * HD)
        top, bottom = slice(g, g + 1), slice(8 + g, 9 + g)
        own_m = st_ref[top, :]
        far_m = jnp.where(valid, fst_ref[top, :], LOWEST)
        highest = jnp.maximum(own_m, far_m)
        own_keep = scaled_to(own_m, highest)
        far_keep = scaled_to(far_m, highest)
        total = st_ref[bottom, :] * own_keep + fst_ref[bottom, :] * far_keep
        mixed = o_ref[cols, :].astype(F32) * own_keep + fo_ref[cols, :].astype(F32) * far_keep
        out_ref[:, cols] = (mixed / total).T.astype(BF16)


def whole_kernel(
    per_step, q_ref, k_ref, v_ref, pk_ref, pv_ref, fk_ref, fv_ref, fpk_ref, fpv_ref, out_ref
):
    index = lax.axis_index("ctx")
    leading = index % 2 == 0
    valid = index >= 2
    beside = jnp.logical_or(valid, jnp.logical_not(leading))
    for g in range(per_step):
        cols = slice(g * HD, (g + 1) * HD)
        other_k = jnp.where(leading, fpk_ref[:, cols], pk_ref[:, cols])
        other_v = jnp.where(leading, fpv_ref[:, cols], pv_ref[:, cols])
        for first in range(0, q_ref.shape[0], CHUNK):
            rows = slice(first, first + CHUNK)
            upto = first + CHUNK
            queries = q_ref[rows, cols]
            own = masked(dot(k_ref[:upto, cols], queries, 1, 1), True, 0, first)
            far = masked(dot(fk_ref[first:, cols], queries, 1, 1), False, first, first)
            own_o, own_m, own_l = soft(own, v_ref[:upto, cols])
            far_o, far_m, far_l = soft(far, fv_ref[first:, cols])
            other_o, other_m, other_l = soft(dot(other_k, queries, 1, 1), other_v)
            far_m = jnp.where(valid, far_m, LOWEST)
            other_m = jnp.where(beside, other_m, LOWEST)
            highest = jnp.maximum(jnp.maximum(own_m, far_m), other_m)
            own_f = scaled_to(own_m, highest)
            far_f = scaled_to(far_m, highest)
            other_f = scaled_to(other_m, highest)
            total = own_l * own_f + far_l * far_f + other_l * other_f
            mixed = own_o * own_f + far_o * far_f + other_o * other_f
            out_ref[rows, cols] = (mixed / total).T.astype(BF16)


def attention_call(kernel, heads, arrays, firsts, outs, units, into=None):
    rows = arrays[0].shape[0] if isinstance(firsts[0], int) else arrays[0].shape[1]
    per_step = max(
        size
        for size in range(1, 6)
        if heads % size == 0 and all(f % size == 0 for f in firsts + outs if isinstance(f, int))
    )

    def spec(first):
        if first == "t":
            return pl.BlockSpec((per_step * HD, rows), lambda i: (i, 0))
        if first == "s":
            return pl.BlockSpec((16, rows), lambda i: (i, 0))
        return pl.BlockSpec((rows, per_step * HD), lambda i: (0, i + first // per_step))

    def shape(first):
        if first == "t":
            return jax.ShapeDtypeStruct((heads * HD, rows), BF16)
        if first == "s":
            return jax.ShapeDtypeStruct((16 * (heads // per_step), rows), F32)
        return jax.ShapeDtypeStruct(into[0], BF16)

    aliases = {}
    in_specs = [spec(first) for first in firsts]
    body = functools.partial(kernel, per_step)
    if into is not None and into[1] is not None:
        aliases = {len(arrays): 0}
        count = len(arrays)
        arrays = list(arrays) + [into[1]]
        in_specs.append(ANY)
        inner = body
        body = lambda *refs: inner(*refs[:count], *refs[count + 1 :])
    return pl.pallas_call(
        body,
        grid=(heads // per_step,),
        in_specs=in_specs,
        out_specs=[spec(first) for first in outs],
        out_shape=[shape(first) for first in outs],
        input_output_aliases=aliases,
        cost_estimate=cost(
            4 * units * rows * rows * heads * HD,
            len(firsts + outs) * rows * heads * HD * 2,
            units * rows * rows * heads,
        ),
    )(*arrays)


def fetch_rows(parts, masks, target, sems):
    index = lax.axis_index("ctx")
    copies = []
    for number, (part, mask) in enumerate(zip(parts, masks)):
        rows = part.shape[0]
        if mask is None:
            place = target
        else:
            place = target.at[pl.ds(pl.multiple_of((index ^ mask) * rows, 32), rows)]
        copy = pltpu.make_async_copy(part, place, sems.at[number])
        copy.start()
        copies.append(copy)
    return copies


def grads_kernel(masks, split, head, *refs):
    count = len(masks)
    key_ref, value_ref, rate_ref = refs[:3]
    parts = refs[3 : 3 + count]
    outs = refs[3 + count : -7]
    low, scaled, hidden, gate_grad, up_grad, update, sems = refs[-7:]
    copies = fetch_rows(parts, masks, low, sems)
    rate = rate_ref[:, head : head + 1]
    scaled[...] = (rate * value_ref[...].astype(F32)).astype(BF16)
    for copy in copies:
        copy.wait()
    tokens = key_ref.shape[0]
    block = min(256, tokens)

    for first in range(0, tokens, block):
        rows = slice(first, first + block)
        keys = key_ref[rows, :]
        gate = dot(keys, low[:, :FD], 1, 1) * INV_ROOT
        up = dot(keys, low[:, FD : 2 * FD], 1, 1) * INV_ROOT
        back = dot(scaled[rows, :], low[:, 2 * FD :], 1, 0) * INV_ROOT
        sigmoid = 1.0 / (1.0 + jnp.exp(-gate))
        silu = gate * sigmoid
        hidden[rows, :] = (silu * up).astype(BF16)
        gate_grad[rows, :] = (back * up * sigmoid * (1.0 + gate * (1.0 - sigmoid))).astype(BF16)
        up_grad[rows, :] = (back * silu).astype(BF16)
    for first in range(0, FD, 128):
        rows = slice(first, first + 128)
        update[rows, :FD] = dot(gate_grad[:, rows], key_ref[...], 0, 0)
        update[rows, FD : 2 * FD] = dot(up_grad[:, rows], key_ref[...], 0, 0)
        update[rows, 2 * FD :] = dot(scaled[:, rows], hidden[...], 0, 0)
    if split:
        index = lax.axis_index("ctx")
        for out, mask in zip(outs, (3, 1, 2, 0)):
            rows = out.shape[0]
            out[...] = update[pl.ds(pl.multiple_of((index ^ mask) * rows, 32), rows), :].astype(out.dtype)
    else:
        outs[0][...] = update[...]


def head_grads(fw_key, fw_value, fw_rate, gathered, head, split):
    tokens = fw_key.shape[0]
    parts = [part for part, _ in gathered]
    masks = [mask for _, mask in gathered]
    column = pl.BlockSpec((tokens, FD), lambda i: (0, head))
    if split:
        rows = parts[0].shape[0]
        out_shape = tuple(jax.ShapeDtypeStruct((rows, SPAN), kind) for kind in (BF16, BF16, F32, F32))
    else:
        out_shape = (jax.ShapeDtypeStruct((FD, SPAN), F32),)
    out_specs = tuple(pl.BlockSpec(out.shape, lambda i: (0, 0)) for out in out_shape)
    return pl.pallas_call(
        functools.partial(grads_kernel, masks, split, head),
        grid=(1,),
        in_specs=[column, column, pl.BlockSpec(fw_rate.shape, lambda i: (0, 0))] + [ANY] * len(parts),
        out_specs=out_specs,
        out_shape=out_shape,
        scratch_shapes=[
            pltpu.VMEM((FD, SPAN), BF16),
            pltpu.VMEM((tokens, FD), BF16),
            pltpu.VMEM((tokens, FD), BF16),
            pltpu.VMEM((tokens, FD), BF16),
            pltpu.VMEM((tokens, FD), BF16),
            pltpu.VMEM((FD, SPAN), F32),
            pltpu.SemaphoreType.DMA((len(parts),)),
        ],
        cost_estimate=cost(12 * tokens * FD * FD, 8e6, tokens * FD),
        name="head_grads",
    )(fw_key, fw_value, fw_rate, *parts)


def move_kernel(sums, w_ref, m_ref, *refs):
    addends = refs[:sums]
    nw_ref, nm_ref, low_ref = refs[-3:]
    update = addends[0][...]
    for addend in addends[1:]:
        update = update + addend[...].astype(F32)
    weights = w_ref[...]
    momentum = DECAY * m_ref[...] + update
    moved = weights + momentum
    nm_ref[...] = momentum
    for part in range(3):
        cols = slice(part * FD, (part + 1) * FD)
        before = jnp.mean(jnp.square(weights[:, cols]), axis=1, keepdims=True)
        after = jnp.mean(jnp.square(moved[:, cols]), axis=1, keepdims=True)
        fresh = moved[:, cols] * (jnp.sqrt(before + EPSILON) * lax.rsqrt(after + EPSILON))
        nw_ref[:, cols] = fresh
        low_ref[:, cols] = fresh.astype(BF16)


def move_weights(fast_weights, momentum, addends, head, previous):
    rows = fast_weights.shape[0]
    block = 32 if rows % 32 == 0 else rows
    wide = pl.BlockSpec((block, SPAN), lambda i: (i, head))
    own = pl.BlockSpec((block, SPAN), lambda i: (i, 0))
    in_specs = [wide, wide] + [own] * len(addends)
    args = [fast_weights, momentum] + list(addends)
    aliases = {}
    if previous is not None:
        aliases = {len(args): 0, len(args) + 1: 1}
        in_specs += [ANY, ANY]
        args += list(previous)
    full = jax.ShapeDtypeStruct(fast_weights.shape, F32)
    return pl.pallas_call(
        functools.partial(move_kernel, len(addends)),
        grid=(rows // block,),
        in_specs=in_specs,
        out_specs=(wide, wide, own),
        out_shape=(full, full, jax.ShapeDtypeStruct((rows, SPAN), BF16)),
        input_output_aliases=aliases,
        cost_estimate=cost(20 * rows * SPAN, 26 * rows * SPAN),
        name="move_weights",
    )(*args)


def query_kernel(masks, q_ref, *refs):
    count = len(masks)
    parts = refs[:count]
    out_ref, low, sems = refs[-3:]
    for copy in fetch_rows(parts, masks, low, sems):
        copy.wait()
    tokens = q_ref.shape[0]
    block = min(256, tokens)

    for first in range(0, tokens, block):
        rows = slice(first, first + block)
        queries = q_ref[rows, :]
        gate = dot(queries, low[:, :FD], 1, 1) * INV_ROOT
        up = dot(queries, low[:, FD : 2 * FD], 1, 1) * INV_ROOT
        hidden = (gate * (1.0 / (1.0 + jnp.exp(-gate))) * up).astype(BF16)
        out_ref[rows, :] = (dot(hidden, low[:, 2 * FD :], 1, 1) * INV_ROOT).astype(BF16)


def head_query(fw_query, gathered, head, previous):
    tokens = fw_query.shape[0]
    parts = [part for part, _ in gathered]
    masks = [mask for _, mask in gathered]
    column = pl.BlockSpec((tokens, FD), lambda i: (0, head))
    in_specs = [column] + [ANY] * len(parts)
    args = [fw_query] + parts
    aliases = {}
    if previous is not None:
        aliases = {len(args): 0}
        in_specs.append(ANY)
        args.append(previous)
    return pl.pallas_call(
        functools.partial(query_kernel, masks),
        grid=(1,),
        in_specs=in_specs,
        out_specs=column,
        out_shape=jax.ShapeDtypeStruct(fw_query.shape, BF16),
        scratch_shapes=[pltpu.VMEM((FD, SPAN), BF16), pltpu.SemaphoreType.DMA((len(parts),))],
        input_output_aliases=aliases,
        cost_estimate=cost(6 * tokens * FD * FD, 4e6, tokens * FD),
        name="head_query",
    )(*args)


def swapped(array, mask):
    devices = lax.axis_size("ctx")
    return lax.ppermute(array, "ctx", [(i, i ^ mask) for i in range(devices)])


def shifted(array, by):
    devices = lax.axis_size("ctx")
    pairs = [(i, i + by) for i in range(devices) if 0 <= i + by < devices]
    return lax.ppermute(array, "ctx", pairs)


def after(array, *others):
    return lax.optimization_barrier((array,) + others)[0]


class Lane:
    def __init__(self):
        self.ended = None

    def cross(self, array):
        if self.ended is not None:
            array = after(array, self.ended)
        self.ended = swapped(array, 2)
        return self.ended


def gather_rows(lane, shard, paired):
    if not paired:
        return [(lax.all_gather(shard, "ctx", axis=0, tiled=True), None)]
    across = lane.cross(shard)
    beside = swapped(shard, 1)
    return [(shard, 0), (beside, 1), (across, 2), (swapped(across, 1), 3)]


def sum_rows(lane, pieces, paired):
    if not paired:
        return [lax.psum_scatter(pieces[0], "ctx", scatter_dimension=0, tiled=True)]
    far, near, across, own = pieces
    far = swapped(far, 1)
    near = swapped(near, 1)
    total = (across + far.astype(F32)).astype(BF16)
    return [own, near, lane.cross(total)]


def per_device(
    attn_query, attn_key, attn_value, fw_query, fw_key, fw_value, fw_rate, fast_weights, momentum
):
    devices = lax.axis_size("ctx")
    head_local = fw_rate.shape[1]
    paired = devices == 4
    lane = Lane()
    heads = range(head_local)
    all_heads = attn_query.shape[1] // HD
    moved = 2 * all_heads // 5
    stay = all_heads - moved

    low = fast_weights[:, :SPAN].astype(BF16)
    gathered = [gather_rows(lane, low, paired)]
    started = gathered[0][2 if paired else 0][0]
    source = after(fast_weights, low)
    for head in heads[1:]:
        low = source[:, head * SPAN : (head + 1) * SPAN].astype(BF16)
        gathered.append(gather_rows(lane, low, paired))

    pair_key = swapped(attn_key, 1)
    pair_value = swapped(attn_value, 1)
    queries = attn_query[:, moved * HD :]
    pairs = jnp.concatenate([attn_key[:, : moved * HD], attn_value[:, : moved * HD]], axis=1)
    far_query = shifted(after(queries, started), -2)
    far_pairs = shifted(after(pairs, started), 2)
    far_pairs_other = swapped(far_pairs, 1)

    own = attention_call(
        own_kernel, stay, [queries, attn_key, attn_value], [0, moved, moved], ["t", "s"], 0.6
    )
    before = own[1]
    sums = []
    for head in heads:
        pieces = head_grads(after(fw_key, before), fw_value, fw_rate, gathered[head], head, paired)
        before = pieces[-1]
        sums.append(sum_rows(lane, pieces, paired))
    far_o, far_st, own_o, own_st = attention_call(
        group_kernel,
        stay,
        [queries, after(far_query, before), attn_key, attn_value, pair_key, pair_value, *own],
        [0, 0, moved, moved, moved, moved, "t", "s"],
        ["t", "s", "t", "s"],
        1.6,
    )
    far_o = shifted(far_o, 2)
    far_st = shifted(far_st, 2)

    new = None
    new_gathered = []
    for head in heads:
        new_weights, new_momentum, low = move_weights(fast_weights, momentum, sums[head], head, new)
        new = (new_weights, new_momentum)
        new_gathered.append(gather_rows(lane, low, paired))
    attn_out = attention_call(
        whole_kernel,
        moved,
        [attn_query, attn_key, attn_value, pair_key, pair_value, far_pairs, far_pairs, far_pairs_other, far_pairs_other],
        [0, 0, 0, 0, 0, 0, moved, 0, moved],
        [0],
        2.2,
        (attn_query.shape, None),
    )[0]
    fw_out = None
    for head in heads:
        fw_out = head_query(fw_query, new_gathered[head], head, fw_out)
    attn_out = attention_call(
        merge_kernel,
        stay,
        [own_o, own_st, far_o, far_st],
        ["t", "s", "t", "s"],
        [moved],
        0.01,
        (attn_query.shape, attn_out),
    )[0]
    return (attn_out, fw_out, new_weights, new_momentum)


def solution(mesh):
    spec = P(("seq", "ctx"), "head")

    return jax.shard_map(
        per_device, mesh=mesh, in_specs=(spec,) * 9, out_specs=(spec,) * 4, check_vma=False
    )
```

```python
import functools
import math

import jax
import jax.numpy as jnp
from jax import lax
from jax.experimental import pallas as pl
from jax.experimental.pallas import tpu as pltpu
from jax.sharding import PartitionSpec as P


HD = 128
FD = 640
EPSILON = 1e-06
DECAY = 0.9
SPAN = 3 * FD
INV_ROOT = FD ** (-0.5)
EXP2_SCALE = HD ** (-0.5) * math.log2(math.e)
LOWEST = -1e30
F32 = jnp.float32
BF16 = jnp.bfloat16
ANY = pl.BlockSpec(memory_space=pltpu.HBM)
PARAMS = pltpu.CompilerParams(vmem_limit_bytes=67043328)


def dot(a, b, a_dim, b_dim):
    return lax.dot_general(a, b, (((a_dim,), (b_dim,)), ((), ())), preferred_element_type=F32)


def cost(flops, bytes_accessed, transcendentals=0):
    return pl.CostEstimate(
        flops=int(flops), bytes_accessed=int(bytes_accessed), transcendentals=int(transcendentals)
    )


CHUNK = 128


def soft(scores, values):
    highest = jnp.max(scores, axis=0, keepdims=True)
    weights = jnp.exp2((scores - highest) * EXP2_SCALE)
    total = jnp.sum(weights, axis=0, keepdims=True)
    return dot(values, weights.astype(BF16), 0, 0), highest, total


def masked(scores, causal, first_key, first_query):
    key_row = lax.broadcasted_iota(jnp.int32, scores.shape, 0) + first_key
    query_row = lax.broadcasted_iota(jnp.int32, scores.shape, 1) + first_query
    allowed = key_row <= query_row if causal else key_row > query_row
    return jnp.where(allowed, scores, LOWEST)


def scaled_to(before, after):
    return jnp.exp2((before - after) * EXP2_SCALE)


def own_kernel(per_step, q_ref, k_ref, v_ref, o_ref, st_ref):
    for g in range(per_step):
        cols = slice(g * HD, (g + 1) * HD)
        for first in range(0, q_ref.shape[0], CHUNK):
            rows = slice(first, first + CHUNK)
            upto = first + CHUNK
            scores = masked(dot(k_ref[:upto, cols], q_ref[rows, cols], 1, 1), True, 0, first)
            mixed, highest, total = soft(scores, v_ref[:upto, cols])
            o_ref[cols, rows] = mixed.astype(BF16)
            st_ref[g : g + 1, rows] = highest
            st_ref[per_step + g : per_step + g + 1, rows] = total


def group_kernel(
    per_step, q_ref, far_ref, k_ref, v_ref, pk_ref, pv_ref, o_ref, st_ref, fo_ref, fst_ref, lo_ref, lst_ref
):
    leading = lax.axis_index("ctx") % 2 == 0
    for g in range(per_step):
        cols = slice(g * HD, (g + 1) * HD)
        top, bottom = slice(g, g + 1), slice(per_step + g, per_step + g + 1)
        for first in range(0, q_ref.shape[0], CHUNK):
            rows = slice(first, first + CHUNK)
            far = far_ref[rows, cols]
            scores = masked(dot(k_ref[first:, cols], far, 1, 1), False, first, first)
            far_o, far_m, far_l = soft(scores, v_ref[first:, cols])
            guest = jnp.where(leading, far, q_ref[rows, cols])
            mixed, highest, total = soft(dot(pk_ref[:, cols], guest, 1, 1), pv_ref[:, cols])
            far_top = jnp.where(leading, jnp.maximum(far_m, highest), far_m)
            far_keep = scaled_to(far_m, far_top)
            far_add = jnp.where(leading, scaled_to(highest, far_top), 0.0)
            fo_ref[cols, rows] = (far_o * far_keep + mixed * far_add).astype(BF16)
            fst_ref[top, rows] = far_top
            fst_ref[bottom, rows] = far_l * far_keep + total * far_add
            own_m = st_ref[top, rows]
            own_top = jnp.where(leading, own_m, jnp.maximum(own_m, highest))
            own_keep = scaled_to(own_m, own_top)
            own_add = jnp.where(leading, 0.0, scaled_to(highest, own_top))
            lo_ref[cols, rows] = (o_ref[cols, rows].astype(F32) * own_keep + mixed * own_add).astype(BF16)
            lst_ref[top, rows] = own_top
            lst_ref[bottom, rows] = st_ref[bottom, rows] * own_keep + total * own_add


def merge_kernel(per_step, o_ref, st_ref, fo_ref, fst_ref, out_ref):
    valid = lax.axis_index("ctx") >= 2
    for g in range(per_step):
        cols = slice(g * HD, (g + 1) * HD)
        top, bottom = slice(g, g + 1), slice(per_step + g, per_step + g + 1)
        own_m = st_ref[top, :]
        far_m = jnp.where(valid, fst_ref[top, :], LOWEST)
        highest = jnp.maximum(own_m, far_m)
        own_keep = scaled_to(own_m, highest)
        far_keep = scaled_to(far_m, highest)
        total = st_ref[bottom, :] * own_keep + fst_ref[bottom, :] * far_keep
        mixed = o_ref[cols, :].astype(F32) * own_keep + fo_ref[cols, :].astype(F32) * far_keep
        out_ref[:, cols] = (mixed / total).T.astype(BF16)


def whole_kernel(
    per_step, q_ref, k_ref, v_ref, pk_ref, pv_ref, fk_ref, fv_ref, fpk_ref, fpv_ref, out_ref
):
    index = lax.axis_index("ctx")
    leading = index % 2 == 0
    valid = index >= 2
    beside = jnp.logical_or(valid, jnp.logical_not(leading))
    for g in range(per_step):
        cols = slice(g * HD, (g + 1) * HD)
        other_k = jnp.where(leading, fpk_ref[:, cols], pk_ref[:, cols])
        other_v = jnp.where(leading, fpv_ref[:, cols], pv_ref[:, cols])
        for first in range(0, q_ref.shape[0], CHUNK):
            rows = slice(first, first + CHUNK)
            upto = first + CHUNK
            queries = q_ref[rows, cols]
            own = masked(dot(k_ref[:upto, cols], queries, 1, 1), True, 0, first)
            far = masked(dot(fk_ref[first:, cols], queries, 1, 1), False, first, first)
            own_o, own_m, own_l = soft(own, v_ref[:upto, cols])
            far_o, far_m, far_l = soft(far, fv_ref[first:, cols])
            other_o, other_m, other_l = soft(dot(other_k, queries, 1, 1), other_v)
            far_m = jnp.where(valid, far_m, LOWEST)
            other_m = jnp.where(beside, other_m, LOWEST)
            highest = jnp.maximum(jnp.maximum(own_m, far_m), other_m)
            own_f = scaled_to(own_m, highest)
            far_f = scaled_to(far_m, highest)
            other_f = scaled_to(other_m, highest)
            total = own_l * own_f + far_l * far_f + other_l * other_f
            mixed = own_o * own_f + far_o * far_f + other_o * other_f
            out_ref[rows, cols] = (mixed / total).T.astype(BF16)


def attention_call(kernel, heads, arrays, firsts, outs, units, into=None, most=5):
    rows = arrays[0].shape[0] if isinstance(firsts[0], int) else arrays[0].shape[1]
    per_step = max(
        size
        for size in range(1, most + 1)
        if heads % size == 0 and all(f % size == 0 for f in firsts + outs if isinstance(f, int))
    )

    stat_rows = 8 * pl.cdiv(2 * per_step, 8)

    def spec(first):
        if first == "t":
            return pl.BlockSpec((per_step * HD, rows), lambda i: (i, 0))
        if first == "s":
            return pl.BlockSpec((stat_rows, rows), lambda i: (i, 0))
        return pl.BlockSpec((rows, per_step * HD), lambda i: (0, i + first // per_step))

    def shape(first):
        if first == "t":
            return jax.ShapeDtypeStruct((heads * HD, rows), BF16)
        if first == "s":
            return jax.ShapeDtypeStruct((stat_rows * (heads // per_step), rows), F32)
        return jax.ShapeDtypeStruct(into[0], BF16)

    aliases = {}
    in_specs = [spec(first) for first in firsts]
    body = functools.partial(kernel, per_step)
    if into is not None and into[1] is not None:
        aliases = {len(arrays): 0}
        count = len(arrays)
        arrays = list(arrays) + [into[1]]
        in_specs.append(ANY)
        inner = body
        body = lambda *refs: inner(*refs[:count], *refs[count + 1 :])
    return pl.pallas_call(
        body,
        grid=(heads // per_step,),
        in_specs=in_specs,
        out_specs=[spec(first) for first in outs],
        out_shape=[shape(first) for first in outs],
        input_output_aliases=aliases,
        compiler_params=PARAMS,
        cost_estimate=cost(
            4 * units * rows * rows * heads * HD,
            len(firsts + outs) * rows * heads * HD * 2,
            units * rows * rows * heads,
        ),
    )(*arrays)


def rows_of(mask, rows):
    return pl.ds(pl.multiple_of((lax.axis_index("ctx") ^ mask) * rows, 32), rows)


class Copies:
    def __init__(self, sems):
        self.sems = sems
        self.used = 0

    def start(self, source, target):
        copy = pltpu.make_async_copy(source, target, self.sems.at[self.used])
        self.used += 1
        copy.start()
        return copy

    def part(self, parts, masks, low, third):
        cols = slice(third * FD, (third + 1) * FD)
        copies = []
        for part, mask in zip(parts, masks):
            rows = part.shape[0]
            place = slice(None) if mask is None else rows_of(mask, rows)
            copies.append(self.start(part.at[:, cols], low.at[place, cols]))
        return copies


def wait(copies):
    for copy in copies:
        copy.wait()


def grads_kernel(masks, split, head, *refs):
    count = len(masks)
    rate_ref, key_hbm, value_hbm = refs[:3]
    parts = refs[3 : 3 + count]
    outs = refs[3 + count : -10]
    key_ref, value_ref, low, scaled, hidden, gate_grad, up_grad, update, stage, sems = refs[-10:]
    mine = slice(head * FD, (head + 1) * FD)
    copies = Copies(sems)
    key_copy = copies.start(key_hbm.at[:, mine], key_ref)
    gate_copies = copies.part(parts, masks, low, 0)
    up_copies = copies.part(parts, masks, low, 1)
    value_copy = copies.start(value_hbm.at[:, mine], value_ref)
    back_copies = copies.part(parts, masks, low, 2)
    tokens = key_ref.shape[0]
    rate = jnp.broadcast_to(rate_ref[head : head + 1, :], (8, tokens)).T[:, :1]
    block = min(256, tokens)
    for first in range(0, tokens, block):
        rows = slice(first, first + block)
        if first == 0:
            wait([key_copy] + gate_copies)
        keys = key_ref[rows, :]
        gate = dot(keys, low[:, :FD], 1, 1) * INV_ROOT
        if first == 0:
            wait(up_copies)
        up = dot(keys, low[:, FD : 2 * FD], 1, 1) * INV_ROOT
        if first == 0:
            wait([value_copy])
            scaled[...] = (rate * value_ref[...].astype(F32)).astype(BF16)
            wait(back_copies)
        back = dot(scaled[rows, :], low[:, 2 * FD :], 1, 0) * INV_ROOT
        sigmoid = 1.0 / (1.0 + jnp.exp(-gate))
        silu = gate * sigmoid
        hidden[rows, :] = (silu * up).astype(BF16)
        gate_grad[rows, :] = (back * up * sigmoid * (1.0 + gate * (1.0 - sigmoid))).astype(BF16)
        up_grad[rows, :] = (back * silu).astype(BF16)
    sent = []
    for third, (left, right) in enumerate(((gate_grad, key_ref), (up_grad, key_ref), (scaled, hidden))):
        cols = slice(third * FD, (third + 1) * FD)
        for first in range(0, FD, 128):
            rows = slice(first, first + 128)
            update[rows, cols] = dot(left[:, rows], right[...], 0, 0)
        if split:
            far, near, across, own = outs
            rows = far.shape[0]
            for number, (out, mask) in enumerate(((far, 3), (near, 1), (across, 2))):
                place = slice(number * rows, (number + 1) * rows)
                stage[place, cols] = update[rows_of(mask, rows), cols].astype(BF16)
                sent.append(copies.start(stage.at[place, cols], out.at[:, cols]))
            sent.append(copies.start(update.at[rows_of(0, rows), cols], own.at[:, cols]))
        else:
            sent.append(copies.start(update.at[:, cols], outs[0].at[:, cols]))
    wait(sent)


def head_grads(fw_key, fw_value, fw_rate, gathered, head, split):
    tokens = fw_key.shape[0]
    parts = [part for part, _ in gathered]
    masks = [mask for _, mask in gathered]
    if split:
        rows = parts[0].shape[0]
        out_shape = tuple(jax.ShapeDtypeStruct((rows, SPAN), kind) for kind in (BF16, BF16, BF16, F32))
    else:
        out_shape = (jax.ShapeDtypeStruct((FD, SPAN), F32),)
    by_token = pltpu.VMEM((tokens, FD), BF16)
    return pl.pallas_call(
        functools.partial(grads_kernel, masks, split, head),
        in_specs=[pl.BlockSpec(memory_space=pltpu.VMEM)] + [ANY] * (2 + len(parts)),
        out_specs=tuple(ANY for _ in out_shape),
        out_shape=out_shape,
        scratch_shapes=[
            by_token,
            by_token,
            pltpu.VMEM((FD, SPAN), BF16),
            by_token,
            by_token,
            by_token,
            by_token,
            pltpu.VMEM((FD, SPAN), F32),
            pltpu.VMEM((3 * parts[0].shape[0] if split else 16, SPAN), BF16),
            pltpu.SemaphoreType.DMA((2 + 3 * len(parts) + 3 * len(out_shape),)),
        ],
        compiler_params=PARAMS,
        cost_estimate=cost(12 * tokens * FD * FD, 8e6, tokens * FD),
        name="head_grads",
    )(fw_rate.T, fw_key, fw_value, *parts)


def round_kernel(w_ref, low_ref):
    low_ref[...] = w_ref[...].astype(BF16)


def row_block(rows, most):
    return max((size for size in range(16, most + 1, 16) if rows % size == 0), default=rows)


def round_head(fast_weights, head):
    rows = fast_weights.shape[0]
    block = row_block(rows, 80)
    return pl.pallas_call(
        round_kernel,
        grid=(rows // block,),
        in_specs=[pl.BlockSpec((block, SPAN), lambda i: (i, head))],
        out_specs=pl.BlockSpec((block, SPAN), lambda i: (i, 0)),
        out_shape=jax.ShapeDtypeStruct((rows, SPAN), BF16),
        compiler_params=PARAMS,
        cost_estimate=cost(rows * SPAN, 6 * rows * SPAN),
        name="round_head",
    )(fast_weights)


def pack_kernel(moved, q_ref, k_ref, v_ref, queries_ref, pairs_ref):
    width = moved * HD
    queries_ref[...] = q_ref[:, width:]
    pairs_ref[:, :width] = k_ref[...]
    pairs_ref[:, width:] = v_ref[...]


def pack_travellers(attn_query, attn_key, attn_value, moved):
    rows, width = attn_query.shape
    block = row_block(rows, 256)

    def spec(cols):
        return pl.BlockSpec((block, cols), lambda i: (i, 0))

    widths = (width - moved * HD, 2 * moved * HD)
    return pl.pallas_call(
        functools.partial(pack_kernel, moved),
        grid=(rows // block,),
        in_specs=[spec(width), spec(moved * HD), spec(moved * HD)],
        out_specs=[spec(cols) for cols in widths],
        out_shape=[jax.ShapeDtypeStruct((rows, cols), BF16) for cols in widths],
        compiler_params=PARAMS,
        cost_estimate=cost(0, 8 * rows * width),
        name="pack_travellers",
    )(attn_query, attn_key, attn_value)


def move_kernel(sums, w_ref, m_ref, *refs):
    addends = refs[:sums]
    nw_ref, nm_ref, low_ref = refs[-3:]
    update = addends[0][...]
    for addend in addends[1:]:
        update = update + addend[...].astype(F32)
    weights = w_ref[...]
    momentum = DECAY * m_ref[...] + update
    moved = weights + momentum
    nm_ref[...] = momentum
    for part in range(3):
        cols = slice(part * FD, (part + 1) * FD)
        before = jnp.mean(jnp.square(weights[:, cols]), axis=1, keepdims=True)
        after = jnp.mean(jnp.square(moved[:, cols]), axis=1, keepdims=True)
        fresh = moved[:, cols] * (jnp.sqrt(before + EPSILON) * lax.rsqrt(after + EPSILON))
        nw_ref[:, cols] = fresh
        low_ref[:, cols] = fresh.astype(BF16)


def move_weights(fast_weights, momentum, addends, head, previous):
    rows = fast_weights.shape[0]
    block = row_block(rows, 80)
    wide = pl.BlockSpec((block, SPAN), lambda i: (i, head))
    own = pl.BlockSpec((block, SPAN), lambda i: (i, 0))
    in_specs = [wide, wide] + [own] * len(addends)
    args = [fast_weights, momentum] + list(addends)
    aliases = {}
    if previous is not None:
        aliases = {len(args): 0, len(args) + 1: 1}
        in_specs += [ANY, ANY]
        args += list(previous)
    full = jax.ShapeDtypeStruct(fast_weights.shape, F32)
    return pl.pallas_call(
        functools.partial(move_kernel, len(addends)),
        grid=(rows // block,),
        in_specs=in_specs,
        out_specs=(wide, wide, own),
        out_shape=(full, full, jax.ShapeDtypeStruct((rows, SPAN), BF16)),
        input_output_aliases=aliases,
        compiler_params=PARAMS,
        cost_estimate=cost(20 * rows * SPAN, 26 * rows * SPAN),
        name="move_weights",
    )(*args)


def query_kernel(masks, q_hbm, head, *refs):
    count = len(masks)
    parts = refs[:count]
    out_hbm, q_ref, low, stage, sems = refs[-5:]
    mine = slice(head * FD, (head + 1) * FD)
    copies = Copies(sems)
    query_copy = copies.start(q_hbm.at[:, mine], q_ref)
    loads = [copies.part(parts, masks, low, third) for third in range(3)]
    tokens = q_ref.shape[0]
    block = min(256, tokens)
    sent = []
    for first in range(0, tokens, block):
        rows = slice(first, first + block)
        if first == 0:
            wait([query_copy] + loads[0])
        queries = q_ref[rows, :]
        gate = dot(queries, low[:, :FD], 1, 1) * INV_ROOT
        if first == 0:
            wait(loads[1])
        up = dot(queries, low[:, FD : 2 * FD], 1, 1) * INV_ROOT
        hidden = (gate * (1.0 / (1.0 + jnp.exp(-gate))) * up).astype(BF16)
        if first == 0:
            wait(loads[2])
        stage[rows, :] = (dot(hidden, low[:, 2 * FD :], 1, 1) * INV_ROOT).astype(BF16)
        sent.append(copies.start(stage.at[rows, :], out_hbm.at[rows, mine]))
    wait(sent)


def head_query(fw_query, gathered, head, previous):
    tokens = fw_query.shape[0]
    parts = [part for part, _ in gathered]
    masks = [mask for _, mask in gathered]
    args = [fw_query] + parts
    aliases = {}
    if previous is not None:
        aliases = {len(args): 0}
        args.append(previous)
    by_token = pltpu.VMEM((tokens, FD), BF16)
    return pl.pallas_call(
        lambda q_hbm, *refs: query_kernel(masks, q_hbm, head, *refs),
        in_specs=[ANY] * len(args),
        out_specs=ANY,
        out_shape=jax.ShapeDtypeStruct(fw_query.shape, BF16),
        scratch_shapes=[
            by_token,
            pltpu.VMEM((FD, SPAN), BF16),
            by_token,
            pltpu.SemaphoreType.DMA((1 + 3 * len(parts) + pl.cdiv(tokens, 256),)),
        ],
        input_output_aliases=aliases,
        compiler_params=PARAMS,
        cost_estimate=cost(6 * tokens * FD * FD, 4e6, tokens * FD),
        name="head_query",
    )(*args)


def swapped(array, mask):
    devices = lax.axis_size("ctx")
    return lax.ppermute(array, "ctx", [(i, i ^ mask) for i in range(devices)])


def shifted(array, by):
    devices = lax.axis_size("ctx")
    pairs = [(i, i + by) for i in range(devices) if 0 <= i + by < devices]
    return lax.ppermute(array, "ctx", pairs)


def after(array, *others):
    return lax.optimization_barrier((array,) + others)[0]


def gather_rows(shard, paired):
    if not paired:
        return [(lax.all_gather(shard, "ctx", axis=0, tiled=True), None)]
    across = swapped(shard, 2)
    beside = swapped(shard, 1)
    return [(shard, 0), (beside, 1), (across, 2), (swapped(across, 1), 3)]


def sum_rows(pieces, paired):
    if not paired:
        return [lax.psum_scatter(pieces[0], "ctx", scatter_dimension=0, tiled=True)]
    far, near, across, own = pieces
    far = swapped(far, 1)
    near = swapped(near, 1)
    total = (across.astype(F32) + far.astype(F32)).astype(BF16)
    return [own, near, swapped(total, 2)]


def per_device(
    attn_query, attn_key, attn_value, fw_query, fw_key, fw_value, fw_rate, fast_weights, momentum
):
    devices = lax.axis_size("ctx")
    head_local = fw_rate.shape[1]
    paired = devices == 4
    heads = range(head_local)
    all_heads = attn_query.shape[1] // HD
    moved = 2 * all_heads // 5
    stay = all_heads - moved

    gathered = []
    source = fast_weights
    for head in heads:
        low = round_head(source, head)
        gathered.append(gather_rows(low if head == 0 else after(low, started), paired))
        if head == 0:
            started = gathered[0][2 if paired else 0][0]
            source = after(fast_weights, low)
    queries, pairs = pack_travellers(after(attn_query, source[:1, :1]), attn_key, attn_value, moved)
    pair_key = swapped(attn_key, 1)
    pair_value = swapped(attn_value, 1)
    far_query = shifted(after(queries, started), -2)
    far_pairs = shifted(after(pairs, started), 2)
    far_pairs_other = swapped(far_pairs, 1)

    own = attention_call(
        own_kernel, stay, [queries, attn_key, attn_value], [0, moved, moved], ["t", "s"], 0.6
    )
    before = own[1]
    sums = []
    for head in heads:
        pieces = head_grads(after(fw_key, before), fw_value, fw_rate, gathered[head], head, paired)
        before = pieces[-1]
        sums.append(sum_rows(pieces, paired))
    far_o, far_st, own_o, own_st = attention_call(
        group_kernel,
        stay,
        [queries, after(far_query, before), attn_key, attn_value, pair_key, pair_value, *own],
        [0, 0, moved, moved, moved, moved, "t", "s"],
        ["t", "s", "t", "s"],
        1.6,
    )

    new = None
    new_gathered = []
    for head in heads:
        new_weights, new_momentum, low = move_weights(fast_weights, momentum, sums[head], head, new)
        new = (new_weights, new_momentum)
        new_gathered.append(gather_rows(low, paired))
        if head == 0:
            far_o = shifted(after(far_o, low), 2)
            far_st = shifted(after(far_st, low), 2)
            attn_out = attention_call(
                whole_kernel,
                moved,
                [after(attn_query, low), attn_key, attn_value, pair_key, pair_value, far_pairs, far_pairs, far_pairs_other, far_pairs_other],
                [0, 0, 0, 0, 0, 0, moved, 0, moved],
                [0],
                2.2,
                (attn_query.shape, None),
                2,
            )[0]
            momentum = after(momentum, attn_out)
    fw_out = None
    for head in heads:
        fw_out = head_query(fw_query, new_gathered[head], head, fw_out)
    attn_out = attention_call(
        merge_kernel,
        stay,
        [own_o, own_st, far_o, far_st],
        ["t", "s", "t", "s"],
        [moved],
        0.01,
        (attn_query.shape, attn_out),
    )[0]
    return (attn_out, fw_out, new_weights, new_momentum)


def solution(mesh):
    spec = P(("seq", "ctx"), "head")

    return jax.shard_map(
        per_device, mesh=mesh, in_specs=(spec,) * 9, out_specs=(spec,) * 4, check_vma=False
    )
```

```python
import functools
import math

import jax
import jax.numpy as jnp
from jax import lax
from jax.experimental import pallas as pl
from jax.experimental.pallas import tpu as pltpu
from jax.sharding import PartitionSpec as P


HD = 128
FD = 640
EPSILON = 1e-06
DECAY = 0.9
SPAN = 3 * FD
INV_ROOT = FD ** (-0.5)
EXP2_SCALE = HD ** (-0.5) * math.log2(math.e)
LOWEST = -1e30
F32 = jnp.float32
BF16 = jnp.bfloat16
ANY = pl.BlockSpec(memory_space=pltpu.HBM)
PARAMS = pltpu.CompilerParams(vmem_limit_bytes=67043328)


def dot(a, b, a_dim, b_dim):
    return lax.dot_general(a, b, (((a_dim,), (b_dim,)), ((), ())), preferred_element_type=F32)


def cost(flops, bytes_accessed, transcendentals=0):
    return pl.CostEstimate(
        flops=int(flops), bytes_accessed=int(bytes_accessed), transcendentals=int(transcendentals)
    )


CHUNK = 128


def soft(scores, values):
    highest = jnp.max(scores, axis=0, keepdims=True)
    weights = jnp.exp2((scores - highest) * EXP2_SCALE)
    total = jnp.sum(weights, axis=0, keepdims=True)
    return dot(values, weights.astype(BF16), 0, 0), highest, total


def masked(scores, causal, first_key, first_query):
    key_row = lax.broadcasted_iota(jnp.int32, scores.shape, 0) + first_key
    query_row = lax.broadcasted_iota(jnp.int32, scores.shape, 1) + first_query
    allowed = key_row <= query_row if causal else key_row > query_row
    return jnp.where(allowed, scores, LOWEST)


def scaled_to(before, after):
    return jnp.exp2((before - after) * EXP2_SCALE)


def own_kernel(per_step, q_ref, k_ref, v_ref, o_ref, st_ref):
    for g in range(per_step):
        cols = slice(g * HD, (g + 1) * HD)
        for first in range(0, q_ref.shape[0], CHUNK):
            rows = slice(first, first + CHUNK)
            upto = first + CHUNK
            scores = masked(dot(k_ref[:upto, cols], q_ref[rows, cols], 1, 1), True, 0, first)
            mixed, highest, total = soft(scores, v_ref[:upto, cols])
            o_ref[cols, rows] = mixed.astype(BF16)
            st_ref[g : g + 1, rows] = highest
            st_ref[per_step + g : per_step + g + 1, rows] = total


def group_kernel(
    per_step, q_ref, far_ref, k_ref, v_ref, pk_ref, pv_ref, o_ref, st_ref, fo_ref, fst_ref, lo_ref, lst_ref
):
    leading = lax.axis_index("ctx") % 2 == 0
    for g in range(per_step):
        cols = slice(g * HD, (g + 1) * HD)
        top, bottom = slice(g, g + 1), slice(per_step + g, per_step + g + 1)
        for first in range(0, q_ref.shape[0], CHUNK):
            rows = slice(first, first + CHUNK)
            far = far_ref[rows, cols]
            scores = masked(dot(k_ref[first:, cols], far, 1, 1), False, first, first)
            far_o, far_m, far_l = soft(scores, v_ref[first:, cols])
            guest = jnp.where(leading, far, q_ref[rows, cols])
            mixed, highest, total = soft(dot(pk_ref[:, cols], guest, 1, 1), pv_ref[:, cols])
            far_top = jnp.where(leading, jnp.maximum(far_m, highest), far_m)
            far_keep = scaled_to(far_m, far_top)
            far_add = jnp.where(leading, scaled_to(highest, far_top), 0.0)
            fo_ref[cols, rows] = (far_o * far_keep + mixed * far_add).astype(BF16)
            fst_ref[top, rows] = far_top
            fst_ref[bottom, rows] = far_l * far_keep + total * far_add
            own_m = st_ref[top, rows]
            own_top = jnp.where(leading, own_m, jnp.maximum(own_m, highest))
            own_keep = scaled_to(own_m, own_top)
            own_add = jnp.where(leading, 0.0, scaled_to(highest, own_top))
            lo_ref[cols, rows] = (o_ref[cols, rows].astype(F32) * own_keep + mixed * own_add).astype(BF16)
            lst_ref[top, rows] = own_top
            lst_ref[bottom, rows] = st_ref[bottom, rows] * own_keep + total * own_add


def merge_kernel(per_step, o_ref, st_ref, fo_ref, fst_ref, out_ref):
    valid = lax.axis_index("ctx") >= 2
    for g in range(per_step):
        cols = slice(g * HD, (g + 1) * HD)
        top, bottom = slice(g, g + 1), slice(per_step + g, per_step + g + 1)
        own_m = st_ref[top, :]
        far_m = jnp.where(valid, fst_ref[top, :], LOWEST)
        highest = jnp.maximum(own_m, far_m)
        own_keep = scaled_to(own_m, highest)
        far_keep = scaled_to(far_m, highest)
        total = st_ref[bottom, :] * own_keep + fst_ref[bottom, :] * far_keep
        mixed = o_ref[cols, :].astype(F32) * own_keep + fo_ref[cols, :].astype(F32) * far_keep
        out_ref[:, cols] = (mixed / total).T.astype(BF16)


def whole_kernel(
    per_step, q_ref, k_ref, v_ref, pk_ref, pv_ref, fk_ref, fv_ref, fpk_ref, fpv_ref, out_ref
):
    index = lax.axis_index("ctx")
    leading = index % 2 == 0
    valid = index >= 2
    beside = jnp.logical_or(valid, jnp.logical_not(leading))
    for g in range(per_step):
        cols = slice(g * HD, (g + 1) * HD)
        other_k = jnp.where(leading, fpk_ref[:, cols], pk_ref[:, cols])
        other_v = jnp.where(leading, fpv_ref[:, cols], pv_ref[:, cols])
        for first in range(0, q_ref.shape[0], CHUNK):
            rows = slice(first, first + CHUNK)
            upto = first + CHUNK
            queries = q_ref[rows, cols]
            own = masked(dot(k_ref[:upto, cols], queries, 1, 1), True, 0, first)
            far = masked(dot(fk_ref[first:, cols], queries, 1, 1), False, first, first)
            own_o, own_m, own_l = soft(own, v_ref[:upto, cols])
            far_o, far_m, far_l = soft(far, fv_ref[first:, cols])
            other_o, other_m, other_l = soft(dot(other_k, queries, 1, 1), other_v)
            far_m = jnp.where(valid, far_m, LOWEST)
            other_m = jnp.where(beside, other_m, LOWEST)
            highest = jnp.maximum(jnp.maximum(own_m, far_m), other_m)
            own_f = scaled_to(own_m, highest)
            far_f = scaled_to(far_m, highest)
            other_f = scaled_to(other_m, highest)
            total = own_l * own_f + far_l * far_f + other_l * other_f
            mixed = own_o * own_f + far_o * far_f + other_o * other_f
            out_ref[rows, cols] = (mixed / total).T.astype(BF16)


def attention_call(kernel, heads, arrays, firsts, outs, units, into=None, most=5):
    firsts, outs = [[f if isinstance(f, tuple) else ("c", f) for f in fs] for fs in (firsts, outs)]
    rows = arrays[0].shape[firsts[0][0] != "c"]
    per_step = max(
        size
        for size in range(1, most + 1)
        if heads % size == 0 and all(f % size == 0 for _, f in firsts + outs)
    )

    stat_rows = 8 * pl.cdiv(2 * per_step, 8)

    def spec(kind, first):
        step = first // per_step
        if kind == "t":
            return pl.BlockSpec((per_step * HD, rows), lambda i: (i + step, 0))
        if kind == "s":
            return pl.BlockSpec((stat_rows, rows), lambda i: (i + step, 0))
        return pl.BlockSpec((rows, per_step * HD), lambda i: (0, i + step))

    def shape(kind):
        if kind == "t":
            return jax.ShapeDtypeStruct((heads * HD, rows), BF16)
        if kind == "s":
            return jax.ShapeDtypeStruct((stat_rows * (heads // per_step), rows), F32)
        return jax.ShapeDtypeStruct(into[0], BF16)

    aliases = {}
    in_specs = [spec(*first) for first in firsts]
    body = functools.partial(kernel, per_step)
    if into is not None and into[1] is not None:
        aliases = {len(arrays): 0}
        count = len(arrays)
        arrays = list(arrays) + [into[1]]
        in_specs.append(ANY)
        inner = body
        body = lambda *refs: inner(*refs[:count], *refs[count + 1 :])
    return pl.pallas_call(
        body,
        grid=(heads // per_step,),
        in_specs=in_specs,
        out_specs=[spec(*first) for first in outs],
        out_shape=[shape(kind) for kind, _ in outs],
        input_output_aliases=aliases,
        compiler_params=PARAMS,
        cost_estimate=cost(
            4 * units * rows * rows * heads * HD,
            len(firsts + outs) * rows * heads * HD * 2,
            units * rows * rows * heads,
        ),
    )(*arrays)


def rows_of(mask, rows):
    return pl.ds(pl.multiple_of((lax.axis_index("ctx") ^ mask) * rows, 32), rows)


class Copies:
    def __init__(self, sems):
        self.sems = sems
        self.used = 0

    def start(self, source, target):
        copy = pltpu.make_async_copy(source, target, self.sems.at[self.used])
        self.used += 1
        copy.start()
        return copy

    def part(self, parts, masks, low, third):
        cols = slice(third * FD, (third + 1) * FD)
        copies = []
        for part, mask in zip(parts, masks):
            rows = part.shape[0]
            place = slice(None) if mask is None else rows_of(mask, rows)
            copies.append(self.start(part.at[:, cols], low.at[place, cols]))
        return copies


def wait(copies):
    for copy in copies:
        copy.wait()


def grads_kernel(masks, split, head, *refs):
    count = len(masks)
    rate_ref, key_hbm, value_hbm = refs[:3]
    parts = refs[3 : 3 + count]
    outs = refs[3 + count : -10]
    key_ref, value_ref, low, scaled, hidden, gate_grad, up_grad, update, stage, sems = refs[-10:]
    mine = slice(head * FD, (head + 1) * FD)
    copies = Copies(sems)
    key_copy = copies.start(key_hbm.at[:, mine], key_ref)
    gate_copies = copies.part(parts, masks, low, 0)
    up_copies = copies.part(parts, masks, low, 1)
    value_copy = copies.start(value_hbm.at[:, mine], value_ref)
    back_copies = copies.part(parts, masks, low, 2)
    tokens = key_ref.shape[0]
    rate = jnp.broadcast_to(rate_ref[head : head + 1, :], (8, tokens)).T[:, :1]
    block = min(256, tokens)
    for first in range(0, tokens, block):
        rows = slice(first, first + block)
        if first == 0:
            wait([key_copy] + gate_copies)
        keys = key_ref[rows, :]
        gate = dot(keys, low[:, :FD], 1, 1) * INV_ROOT
        if first == 0:
            wait(up_copies)
        up = dot(keys, low[:, FD : 2 * FD], 1, 1) * INV_ROOT
        if first == 0:
            wait([value_copy])
            scaled[...] = (rate * value_ref[...].astype(F32)).astype(BF16)
            wait(back_copies)
        back = dot(scaled[rows, :], low[:, 2 * FD :], 1, 0) * INV_ROOT
        sigmoid = 1.0 / (1.0 + jnp.exp(-gate))
        silu = gate * sigmoid
        hidden[rows, :] = (silu * up).astype(BF16)
        gate_grad[rows, :] = (back * up * sigmoid * (1.0 + gate * (1.0 - sigmoid))).astype(BF16)
        up_grad[rows, :] = (back * silu).astype(BF16)
    sent = []
    for third, (left, right) in enumerate(((gate_grad, key_ref), (up_grad, key_ref), (scaled, hidden))):
        cols = slice(third * FD, (third + 1) * FD)
        for first in range(0, FD, 128):
            rows = slice(first, first + 128)
            update[rows, cols] = dot(left[:, rows], right[...], 0, 0)
        if split:
            far, near, across, own = outs
            rows = far.shape[0]
            for number, (out, mask) in enumerate(((far, 3), (near, 1), (across, 2))):
                place = slice(number * rows, (number + 1) * rows)
                stage[place, cols] = update[rows_of(mask, rows), cols].astype(BF16)
                sent.append(copies.start(stage.at[place, cols], out.at[:, cols]))
            sent.append(copies.start(update.at[rows_of(0, rows), cols], own.at[:, cols]))
        else:
            sent.append(copies.start(update.at[:, cols], outs[0].at[:, cols]))
    wait(sent)


def head_grads(fw_key, fw_value, fw_rate, gathered, head, split):
    tokens = fw_key.shape[0]
    parts = [part for part, _ in gathered]
    masks = [mask for _, mask in gathered]
    if split:
        rows = parts[0].shape[0]
        out_shape = tuple(jax.ShapeDtypeStruct((rows, SPAN), kind) for kind in (BF16, BF16, BF16, F32))
    else:
        out_shape = (jax.ShapeDtypeStruct((FD, SPAN), F32),)
    by_token = pltpu.VMEM((tokens, FD), BF16)
    return pl.pallas_call(
        functools.partial(grads_kernel, masks, split, head),
        in_specs=[pl.BlockSpec(memory_space=pltpu.VMEM)] + [ANY] * (2 + len(parts)),
        out_specs=tuple(ANY for _ in out_shape),
        out_shape=out_shape,
        scratch_shapes=[
            by_token,
            by_token,
            pltpu.VMEM((FD, SPAN), BF16),
            by_token,
            by_token,
            by_token,
            by_token,
            pltpu.VMEM((FD, SPAN), F32),
            pltpu.VMEM((3 * parts[0].shape[0] if split else 16, SPAN), BF16),
            pltpu.SemaphoreType.DMA((2 + 3 * len(parts) + 3 * len(out_shape),)),
        ],
        compiler_params=PARAMS,
        cost_estimate=cost(12 * tokens * FD * FD, 8e6, tokens * FD),
        name="head_grads",
    )(fw_rate.T, fw_key, fw_value, *parts)


def round_kernel(w_ref, low_ref):
    low_ref[...] = w_ref[...].astype(BF16)


def row_block(rows, most):
    return max((size for size in range(16, most + 1, 16) if rows % size == 0), default=rows)


def round_head(fast_weights, head):
    rows = fast_weights.shape[0]
    block = row_block(rows, 80)
    return pl.pallas_call(
        round_kernel,
        grid=(rows // block,),
        in_specs=[pl.BlockSpec((block, SPAN), lambda i: (i, head))],
        out_specs=pl.BlockSpec((block, SPAN), lambda i: (i, 0)),
        out_shape=jax.ShapeDtypeStruct((rows, SPAN), BF16),
        compiler_params=PARAMS,
        cost_estimate=cost(rows * SPAN, 6 * rows * SPAN),
        name="round_head",
    )(fast_weights)


def pack_kernel(q_ref, k_ref, v_ref, queries_ref, pairs_ref):
    width = k_ref.shape[1]
    queries_ref[...] = q_ref[...]
    pairs_ref[:, :width] = k_ref[...]
    pairs_ref[:, width:] = v_ref[...]


def pack_travellers(attn_query, attn_key, attn_value, stay):
    rows, width = attn_query.shape
    block = row_block(rows, 256)
    left, right = stay * HD, width - stay * HD

    def spec(cols, first=0):
        return pl.BlockSpec((block, cols), lambda i: (i, first // cols))

    widths = (left, 2 * right)
    return pl.pallas_call(
        pack_kernel,
        grid=(rows // block,),
        in_specs=[spec(left), spec(right, left), spec(right, left)],
        out_specs=[spec(cols) for cols in widths],
        out_shape=[jax.ShapeDtypeStruct((rows, cols), BF16) for cols in widths],
        compiler_params=PARAMS,
        cost_estimate=cost(0, 8 * rows * width),
        name="pack_travellers",
    )(attn_query, attn_key, attn_value)


def move_kernel(sums, w_ref, m_ref, *refs):
    addends = refs[:sums]
    nw_ref, nm_ref, low_ref = refs[-3:]
    update = addends[0][...]
    for addend in addends[1:]:
        update = update + addend[...].astype(F32)
    weights = w_ref[...]
    momentum = DECAY * m_ref[...] + update
    moved = weights + momentum
    nm_ref[...] = momentum
    for part in range(3):
        cols = slice(part * FD, (part + 1) * FD)
        before = jnp.mean(jnp.square(weights[:, cols]), axis=1, keepdims=True)
        after = jnp.mean(jnp.square(moved[:, cols]), axis=1, keepdims=True)
        fresh = moved[:, cols] * (jnp.sqrt(before + EPSILON) * lax.rsqrt(after + EPSILON))
        nw_ref[:, cols] = fresh
        low_ref[:, cols] = fresh.astype(BF16)


def move_weights(fast_weights, momentum, addends, head, previous):
    rows = fast_weights.shape[0]
    block = row_block(rows, 80)
    wide = pl.BlockSpec((block, SPAN), lambda i: (i, head))
    own = pl.BlockSpec((block, SPAN), lambda i: (i, 0))
    in_specs = [wide, wide] + [own] * len(addends)
    args = [fast_weights, momentum] + list(addends)
    aliases = {}
    if previous is not None:
        aliases = {len(args): 0, len(args) + 1: 1}
        in_specs += [ANY, ANY]
        args += list(previous)
    full = jax.ShapeDtypeStruct(fast_weights.shape, F32)
    return pl.pallas_call(
        functools.partial(move_kernel, len(addends)),
        grid=(rows // block,),
        in_specs=in_specs,
        out_specs=(wide, wide, own),
        out_shape=(full, full, jax.ShapeDtypeStruct((rows, SPAN), BF16)),
        input_output_aliases=aliases,
        compiler_params=PARAMS,
        cost_estimate=cost(20 * rows * SPAN, 26 * rows * SPAN),
        name="move_weights",
    )(*args)


def query_kernel(masks, q_hbm, head, *refs):
    count = len(masks)
    parts = refs[:count]
    out_hbm, q_ref, low, stage, sems = refs[-5:]
    mine = slice(head * FD, (head + 1) * FD)
    copies = Copies(sems)
    query_copy = copies.start(q_hbm.at[:, mine], q_ref)
    loads = [copies.part(parts, masks, low, third) for third in range(3)]
    tokens = q_ref.shape[0]
    block = min(256, tokens)
    sent = []
    for first in range(0, tokens, block):
        rows = slice(first, first + block)
        if first == 0:
            wait([query_copy] + loads[0])
        queries = q_ref[rows, :]
        gate = dot(queries, low[:, :FD], 1, 1) * INV_ROOT
        if first == 0:
            wait(loads[1])
        up = dot(queries, low[:, FD : 2 * FD], 1, 1) * INV_ROOT
        hidden = (gate * (1.0 / (1.0 + jnp.exp(-gate))) * up).astype(BF16)
        if first == 0:
            wait(loads[2])
        stage[rows, :] = (dot(hidden, low[:, 2 * FD :], 1, 1) * INV_ROOT).astype(BF16)
        sent.append(copies.start(stage.at[rows, :], out_hbm.at[rows, mine]))
    wait(sent)


def head_query(fw_query, gathered, head, previous):
    tokens = fw_query.shape[0]
    parts = [part for part, _ in gathered]
    masks = [mask for _, mask in gathered]
    args = [fw_query] + parts
    aliases = {}
    if previous is not None:
        aliases = {len(args): 0}
        args.append(previous)
    by_token = pltpu.VMEM((tokens, FD), BF16)
    return pl.pallas_call(
        lambda q_hbm, *refs: query_kernel(masks, q_hbm, head, *refs),
        in_specs=[ANY] * len(args),
        out_specs=ANY,
        out_shape=jax.ShapeDtypeStruct(fw_query.shape, BF16),
        scratch_shapes=[
            by_token,
            pltpu.VMEM((FD, SPAN), BF16),
            by_token,
            pltpu.SemaphoreType.DMA((1 + 3 * len(parts) + pl.cdiv(tokens, 256),)),
        ],
        input_output_aliases=aliases,
        compiler_params=PARAMS,
        cost_estimate=cost(6 * tokens * FD * FD, 4e6, tokens * FD),
        name="head_query",
    )(*args)


def swapped(array, mask):
    devices = lax.axis_size("ctx")
    return lax.ppermute(array, "ctx", [(i, i ^ mask) for i in range(devices)])


def shifted(array, by):
    devices = lax.axis_size("ctx")
    pairs = [(i, i + by) for i in range(devices) if 0 <= i + by < devices]
    return lax.ppermute(array, "ctx", pairs)


def after(array, *others):
    return lax.optimization_barrier((array,) + others)[0]


def gather_rows(shard, paired):
    if not paired:
        return [(lax.all_gather(shard, "ctx", axis=0, tiled=True), None)]
    across = swapped(shard, 2)
    beside = swapped(shard, 1)
    return [(shard, 0), (beside, 1), (across, 2), (swapped(across, 1), 3)]


def sum_rows(pieces, paired):
    if not paired:
        return [lax.psum_scatter(pieces[0], "ctx", scatter_dimension=0, tiled=True)], pieces[0]
    far, near, across, own = pieces
    far = swapped(far, 1)
    near = swapped(near, 1)
    total = (across.astype(F32) + far.astype(F32)).astype(BF16)
    return [own, near, swapped(total, 2)], total


def per_device(
    attn_query, attn_key, attn_value, fw_query, fw_key, fw_value, fw_rate, fast_weights, momentum
):
    devices = lax.axis_size("ctx")
    head_local = fw_rate.shape[1]
    paired = devices == 4
    heads = range(head_local)
    all_heads = attn_query.shape[1] // HD
    moved = max(1, all_heads // 5)
    while all_heads % moved:
        moved -= 1
    stay = all_heads - moved
    half = stay // 2 if stay % 2 == 0 else stay
    halves = range(0, stay, half)

    low = round_head(fast_weights, 0)
    gathered = [gather_rows(low, paired)]
    started = gathered[0][2 if paired else 0][0]
    own = attention_call(
        own_kernel,
        stay,
        [after(attn_query, low), attn_key, attn_value],
        [0, 0, 0],
        [("t", 0), ("s", 0)],
        0.6,
        most=half,
    )
    before = own[1]
    for head in heads[1:]:
        low = round_head(after(fast_weights, before), head)
        before = low
        gathered.append(gather_rows(after(low, started), paired))
    queries, pairs = pack_travellers(after(attn_query, before), attn_key, attn_value, stay)
    far_query = shifted(queries, -2)
    far_pairs = shifted(pairs, 2)
    far_pairs_other = swapped(far_pairs, 1)
    pair_key = swapped(attn_key, 1)
    pair_value = swapped(attn_value, 1)

    before = queries
    sums = []
    totals = []
    for head in heads:
        pieces = head_grads(after(fw_key, before), fw_value, fw_rate, gathered[head], head, paired)
        before = pieces[-1]
        addends, total = sum_rows(pieces, paired)
        sums.append(addends)
        totals.append(total)
    found = []
    for first in halves:
        found.append(
            attention_call(
                group_kernel,
                half,
                [
                    attn_query,
                    after(far_query, before),
                    attn_key,
                    attn_value,
                    pair_key,
                    pair_value,
                    *own,
                ],
                [first] * 6 + [("t", first), ("s", first)],
                [("t", 0), ("s", 0), ("t", 0), ("s", 0)],
                1.6,
                most=half,
            )
        )
        before = after(found[-1][1], totals[-1])

    fw_new = None
    new_gathered = []
    for head in heads:
        new_weights, new_momentum, low = move_weights(
            fast_weights, momentum, sums[head], head, fw_new
        )
        fw_new = (new_weights, new_momentum)
        new_gathered.append(gather_rows(low, paired))
        if head == 0:
            attn_out = attention_call(
                whole_kernel,
                moved,
                [
                    after(attn_query, low),
                    attn_key,
                    attn_value,
                    pair_key,
                    pair_value,
                    far_pairs,
                    far_pairs,
                    far_pairs_other,
                    far_pairs_other,
                ],
                [stay] * 5 + [0, moved, 0, moved],
                [stay],
                2.2,
                (attn_query.shape, None),
                most=2,
            )[0]
            momentum = after(momentum, attn_out)
    returned = []
    for number, (far_o, far_st, own_o, own_st) in enumerate(found):
        if number > 0:
            far_o, far_st = after(far_o, low), after(far_st, low)
        returned.append((own_o, own_st, shifted(far_o, 2), shifted(far_st, 2)))
    fw_out = None
    for head in heads:
        fw_out = head_query(fw_query, new_gathered[head], head, fw_out)
    for number, states in enumerate(returned):
        attn_out = attention_call(
            merge_kernel,
            half,
            states,
            [("t", 0), ("s", 0), ("t", 0), ("s", 0)],
            [number * half],
            0.01,
            (attn_query.shape, attn_out),
            most=half,
        )[0]
    return (attn_out, fw_out, new_weights, new_momentum)


def solution(mesh):
    spec = P(("seq", "ctx"), "head")

    return jax.shard_map(
        per_device, mesh=mesh, in_specs=(spec,) * 9, out_specs=(spec,) * 4, check_vma=False
    )
```

```python
import functools
import math

import jax
import jax.numpy as jnp
from jax import lax
from jax.experimental import pallas as pl
from jax.experimental.pallas import tpu as pltpu
from jax.sharding import PartitionSpec as P


HD = 128
FD = 640
EPSILON = 1e-06
DECAY = 0.9
SPAN = 3 * FD
INV_ROOT = FD ** (-0.5)
EXP2_SCALE = HD ** (-0.5) * math.log2(math.e)
LOWEST = -1e30
F32 = jnp.float32
BF16 = jnp.bfloat16
ANY = pl.BlockSpec(memory_space=pltpu.HBM)
PARAMS = pltpu.CompilerParams(vmem_limit_bytes=67043328)


def dot(a, b, a_dim, b_dim):
    return lax.dot_general(a, b, (((a_dim,), (b_dim,)), ((), ())), preferred_element_type=F32)


def cost(flops, bytes_accessed, transcendentals=0):
    return pl.CostEstimate(
        flops=int(flops), bytes_accessed=int(bytes_accessed), transcendentals=int(transcendentals)
    )


CHUNK = 128


def soft(scores, values):
    highest = jnp.max(scores, axis=0, keepdims=True)
    weights = jnp.exp2((scores - highest) * EXP2_SCALE)
    total = jnp.sum(weights, axis=0, keepdims=True)
    return dot(values, weights.astype(BF16), 0, 0), highest, total


def masked(scores, causal, first_key, first_query):
    key_row = lax.broadcasted_iota(jnp.int32, scores.shape, 0) + first_key
    query_row = lax.broadcasted_iota(jnp.int32, scores.shape, 1) + first_query
    allowed = key_row <= query_row if causal else key_row > query_row
    return jnp.where(allowed, scores, LOWEST)


def scaled_to(before, after):
    return jnp.exp2((before - after) * EXP2_SCALE)


def own_kernel(per_step, q_ref, k_ref, v_ref, o_ref, st_ref):
    for g in range(per_step):
        cols = slice(g * HD, (g + 1) * HD)
        for first in range(0, q_ref.shape[0], CHUNK):
            rows = slice(first, first + CHUNK)
            upto = first + CHUNK
            scores = masked(dot(k_ref[:upto, cols], q_ref[rows, cols], 1, 1), True, 0, first)
            mixed, highest, total = soft(scores, v_ref[:upto, cols])
            o_ref[cols, rows] = mixed.astype(BF16)
            st_ref[g : g + 1, rows] = highest
            st_ref[per_step + g : per_step + g + 1, rows] = total


def pieces_of(value, count):
    rows = []
    for _ in range(count):
        rows.append(value.astype(BF16).astype(F32))
        value = value - rows[-1]
    return rows


def stat_places(per_step):
    return 16 * pl.cdiv(5 * per_step, 16)


def group_kernel(
    per_step, q_ref, far_ref, k_ref, v_ref, pk_ref, pv_ref, o_ref, st_ref, fo_ref, lo_ref, lst_ref
):
    leading = lax.axis_index("ctx") % 2 == 0
    places = stat_places(per_step)
    for first in range(0, q_ref.shape[0], CHUNK):
        rows = slice(first, first + CHUNK)
        stats = []
        for g in range(per_step):
            cols = slice(g * HD, (g + 1) * HD)
            top, bottom = slice(g, g + 1), slice(per_step + g, per_step + g + 1)
            far = far_ref[rows, cols]
            scores = masked(dot(k_ref[first:, cols], far, 1, 1), False, first, first)
            far_o, far_m, far_l = soft(scores, v_ref[first:, cols])
            guest = jnp.where(leading, far, q_ref[rows, cols])
            mixed, highest, total = soft(dot(pk_ref[:, cols], guest, 1, 1), pv_ref[:, cols])
            far_top = jnp.where(leading, jnp.maximum(far_m, highest), far_m)
            far_keep = scaled_to(far_m, far_top)
            far_add = jnp.where(leading, scaled_to(highest, far_top), 0.0)
            fo_ref[cols, rows] = (far_o * far_keep + mixed * far_add).astype(BF16)
            stats += pieces_of(far_top, 3) + pieces_of(far_l * far_keep + total * far_add, 2)
            own_m = st_ref[top, rows]
            own_top = jnp.where(leading, own_m, jnp.maximum(own_m, highest))
            own_keep = scaled_to(own_m, own_top)
            own_add = jnp.where(leading, 0.0, scaled_to(highest, own_top))
            lo_ref[cols, rows] = (o_ref[cols, rows].astype(F32) * own_keep + mixed * own_add).astype(BF16)
            lst_ref[top, rows] = own_top
            lst_ref[bottom, rows] = st_ref[bottom, rows] * own_keep + total * own_add
        stats += [jnp.zeros_like(stats[0])] * (places - len(stats))
        fo_ref[per_step * HD :, rows] = jnp.concatenate(stats, axis=0).astype(BF16)


def merge_kernel(per_step, o_ref, st_ref, fo_ref, out_ref):
    valid = lax.axis_index("ctx") >= 2
    stats = fo_ref[per_step * HD :, :].astype(F32)
    for g in range(per_step):
        cols = slice(g * HD, (g + 1) * HD)
        top, bottom = slice(g, g + 1), slice(per_step + g, per_step + g + 1)
        m0, m1, m2, l0, l1 = [stats[5 * g + i : 5 * g + i + 1, :] for i in range(5)]
        own_m = st_ref[top, :]
        far_m = jnp.where(valid, m0 + m1 + m2, LOWEST)
        highest = jnp.maximum(own_m, far_m)
        own_keep = scaled_to(own_m, highest)
        far_keep = scaled_to(far_m, highest)
        total = st_ref[bottom, :] * own_keep + (l0 + l1) * far_keep
        mixed = o_ref[cols, :].astype(F32) * own_keep + fo_ref[cols, :].astype(F32) * far_keep
        out_ref[:, cols] = (mixed / total).T.astype(BF16)


def whole_kernel(
    per_step, q_ref, k_ref, v_ref, pk_ref, pv_ref, fk_ref, fv_ref, fpk_ref, fpv_ref, out_ref
):
    index = lax.axis_index("ctx")
    leading = index % 2 == 0
    valid = index >= 2
    beside = jnp.logical_or(valid, jnp.logical_not(leading))
    for g in range(per_step):
        cols = slice(g * HD, (g + 1) * HD)
        other_k = jnp.where(leading, fpk_ref[:, cols], pk_ref[:, cols])
        other_v = jnp.where(leading, fpv_ref[:, cols], pv_ref[:, cols])
        for first in range(0, q_ref.shape[0], CHUNK):
            rows = slice(first, first + CHUNK)
            upto = first + CHUNK
            queries = q_ref[rows, cols]
            own = masked(dot(k_ref[:upto, cols], queries, 1, 1), True, 0, first)
            far = masked(dot(fk_ref[first:, cols], queries, 1, 1), False, first, first)
            own_o, own_m, own_l = soft(own, v_ref[:upto, cols])
            far_o, far_m, far_l = soft(far, fv_ref[first:, cols])
            other_o, other_m, other_l = soft(dot(other_k, queries, 1, 1), other_v)
            far_m = jnp.where(valid, far_m, LOWEST)
            other_m = jnp.where(beside, other_m, LOWEST)
            highest = jnp.maximum(jnp.maximum(own_m, far_m), other_m)
            own_f = scaled_to(own_m, highest)
            far_f = scaled_to(far_m, highest)
            other_f = scaled_to(other_m, highest)
            total = own_l * own_f + far_l * far_f + other_l * other_f
            mixed = own_o * own_f + far_o * far_f + other_o * other_f
            out_ref[rows, cols] = (mixed / total).T.astype(BF16)


def attention_call(kernel, heads, arrays, firsts, outs, units, into=None, most=5):
    firsts, outs = [[f if isinstance(f, tuple) else ("c", f) for f in fs] for fs in (firsts, outs)]
    rows = arrays[0].shape[firsts[0][0] != "c"]
    per_step = max(
        size
        for size in range(1, most + 1)
        if heads % size == 0 and all(f % size == 0 for _, f in firsts + outs)
    )

    stat_rows = 8 * pl.cdiv(2 * per_step, 8)
    far_rows = per_step * HD + stat_places(per_step)

    def spec(kind, first):
        step = first // per_step
        if kind == "t":
            return pl.BlockSpec((per_step * HD, rows), lambda i: (i + step, 0))
        if kind == "s":
            return pl.BlockSpec((stat_rows, rows), lambda i: (i + step, 0))
        if kind == "f":
            return pl.BlockSpec((far_rows, rows), lambda i: (i + step, 0))
        return pl.BlockSpec((rows, per_step * HD), lambda i: (0, i + step))

    def shape(kind):
        if kind == "t":
            return jax.ShapeDtypeStruct((heads * HD, rows), BF16)
        if kind == "f":
            return jax.ShapeDtypeStruct((far_rows * (heads // per_step), rows), BF16)
        if kind == "s":
            return jax.ShapeDtypeStruct((stat_rows * (heads // per_step), rows), F32)
        return jax.ShapeDtypeStruct(into[0], BF16)

    aliases = {}
    in_specs = [spec(*first) for first in firsts]
    body = functools.partial(kernel, per_step)
    if into is not None and into[1] is not None:
        aliases = {len(arrays): 0}
        count = len(arrays)
        arrays = list(arrays) + [into[1]]
        in_specs.append(ANY)
        inner = body
        body = lambda *refs: inner(*refs[:count], *refs[count + 1 :])
    return pl.pallas_call(
        body,
        grid=(heads // per_step,),
        in_specs=in_specs,
        out_specs=[spec(*first) for first in outs],
        out_shape=[shape(kind) for kind, _ in outs],
        input_output_aliases=aliases,
        compiler_params=PARAMS,
        cost_estimate=cost(
            4 * units * rows * rows * heads * HD,
            len(firsts + outs) * rows * heads * HD * 2,
            units * rows * rows * heads,
        ),
    )(*arrays)


def rows_of(mask, rows):
    return pl.ds(pl.multiple_of((lax.axis_index("ctx") ^ mask) * rows, 32), rows)


class Copies:
    def __init__(self, sems):
        self.sems = sems
        self.used = 0

    def start(self, source, target):
        copy = pltpu.make_async_copy(source, target, self.sems.at[self.used])
        self.used += 1
        copy.start()
        return copy

    def part(self, parts, masks, low, third):
        cols = slice(third * FD, (third + 1) * FD)
        copies = []
        for part, mask in zip(parts, masks):
            rows = part.shape[0]
            place = slice(None) if mask is None else rows_of(mask, rows)
            copies.append(self.start(part.at[:, cols], low.at[place, cols]))
        return copies


def wait(copies):
    for copy in copies:
        copy.wait()


def grads_kernel(masks, split, head, *refs):
    count = len(masks)
    rate_ref, key_hbm, value_hbm = refs[:3]
    parts = refs[3 : 3 + count]
    outs = refs[3 + count : -10]
    key_ref, value_ref, low, scaled, hidden, gate_grad, up_grad, update, stage, sems = refs[-10:]
    mine = slice(head * FD, (head + 1) * FD)
    copies = Copies(sems)
    key_copy = copies.start(key_hbm.at[:, mine], key_ref)
    gate_copies = copies.part(parts, masks, low, 0)
    up_copies = copies.part(parts, masks, low, 1)
    value_copy = copies.start(value_hbm.at[:, mine], value_ref)
    back_copies = copies.part(parts, masks, low, 2)
    tokens = key_ref.shape[0]
    rate = jnp.broadcast_to(rate_ref[head : head + 1, :], (8, tokens)).T[:, :1]
    block = min(256, tokens)
    for first in range(0, tokens, block):
        rows = slice(first, first + block)
        if first == 0:
            wait([key_copy] + gate_copies)
        keys = key_ref[rows, :]
        gate = dot(keys, low[:, :FD], 1, 1) * INV_ROOT
        if first == 0:
            wait(up_copies)
        up = dot(keys, low[:, FD : 2 * FD], 1, 1) * INV_ROOT
        if first == 0:
            wait([value_copy])
            scaled[...] = (rate * value_ref[...].astype(F32)).astype(BF16)
            wait(back_copies)
        back = dot(scaled[rows, :], low[:, 2 * FD :], 1, 0) * INV_ROOT
        sigmoid = 1.0 / (1.0 + jnp.exp(-gate))
        silu = gate * sigmoid
        hidden[rows, :] = (silu * up).astype(BF16)
        gate_grad[rows, :] = (back * up * sigmoid * (1.0 + gate * (1.0 - sigmoid))).astype(BF16)
        up_grad[rows, :] = (back * silu).astype(BF16)
    sent = []
    for third, (left, right) in enumerate(((gate_grad, key_ref), (up_grad, key_ref), (scaled, hidden))):
        cols = slice(third * FD, (third + 1) * FD)
        for first in range(0, FD, 128):
            rows = slice(first, first + 128)
            update[rows, cols] = dot(left[:, rows], right[...], 0, 0)
        if split:
            far, near, across, own = outs
            rows = far.shape[0]
            for number, (out, mask) in enumerate(((far, 3), (near, 1), (across, 2))):
                place = slice(number * rows, (number + 1) * rows)
                stage[place, cols] = update[rows_of(mask, rows), cols].astype(BF16)
                sent.append(copies.start(stage.at[place, cols], out.at[:, cols]))
            sent.append(copies.start(update.at[rows_of(0, rows), cols], own.at[:, cols]))
        else:
            sent.append(copies.start(update.at[:, cols], outs[0].at[:, cols]))
    wait(sent)


def head_grads(fw_key, fw_value, fw_rate, gathered, head, split):
    tokens = fw_key.shape[0]
    parts = [part for part, _ in gathered]
    masks = [mask for _, mask in gathered]
    if split:
        rows = parts[0].shape[0]
        out_shape = tuple(jax.ShapeDtypeStruct((rows, SPAN), kind) for kind in (BF16, BF16, BF16, F32))
    else:
        out_shape = (jax.ShapeDtypeStruct((FD, SPAN), F32),)
    by_token = pltpu.VMEM((tokens, FD), BF16)
    return pl.pallas_call(
        functools.partial(grads_kernel, masks, split, head),
        in_specs=[pl.BlockSpec(memory_space=pltpu.VMEM)] + [ANY] * (2 + len(parts)),
        out_specs=tuple(ANY for _ in out_shape),
        out_shape=out_shape,
        scratch_shapes=[
            by_token,
            by_token,
            pltpu.VMEM((FD, SPAN), BF16),
            by_token,
            by_token,
            by_token,
            by_token,
            pltpu.VMEM((FD, SPAN), F32),
            pltpu.VMEM((3 * parts[0].shape[0] if split else 16, SPAN), BF16),
            pltpu.SemaphoreType.DMA((2 + 3 * len(parts) + 3 * len(out_shape),)),
        ],
        compiler_params=PARAMS,
        cost_estimate=cost(12 * tokens * FD * FD, 8e6, tokens * FD),
        name="head_grads",
    )(fw_rate.T, fw_key, fw_value, *parts)


def add_kernel(left_ref, right_ref, sum_ref):
    sum_ref[...] = (left_ref[...].astype(F32) + right_ref[...].astype(F32)).astype(BF16)


def add_rows(left, right):
    rows, width = left.shape
    block = row_block(rows, 80)
    spec = pl.BlockSpec((block, width), lambda i: (i, 0))
    return pl.pallas_call(
        add_kernel,
        grid=(rows // block,),
        in_specs=[spec, spec],
        out_specs=spec,
        out_shape=jax.ShapeDtypeStruct((rows, width), BF16),
        compiler_params=PARAMS,
        cost_estimate=cost(rows * width, 6 * rows * width),
        name="add_rows",
    )(left, right)


def round_kernel(w_ref, low_ref):
    low_ref[...] = w_ref[...].astype(BF16)


def row_block(rows, most):
    return max((size for size in range(16, most + 1, 16) if rows % size == 0), default=rows)


def round_head(fast_weights, head):
    rows = fast_weights.shape[0]
    block = row_block(rows, 80)
    return pl.pallas_call(
        round_kernel,
        grid=(rows // block,),
        in_specs=[pl.BlockSpec((block, SPAN), lambda i: (i, head))],
        out_specs=pl.BlockSpec((block, SPAN), lambda i: (i, 0)),
        out_shape=jax.ShapeDtypeStruct((rows, SPAN), BF16),
        compiler_params=PARAMS,
        cost_estimate=cost(rows * SPAN, 6 * rows * SPAN),
        name="round_head",
    )(fast_weights)


def pack_kernel(q_ref, k_ref, v_ref, queries_ref, pairs_ref):
    first, width = queries_ref.shape[1], pairs_ref.shape[1] // 2
    queries_ref[...] = q_ref[...]
    pairs_ref[:, :width] = k_ref[:, first:]
    pairs_ref[:, width:] = v_ref[:, first:]


def pack_travellers(attn_query, attn_key, attn_value, stay):
    rows, width = attn_query.shape
    block = row_block(rows, 256)
    left, right = stay * HD, width - stay * HD

    def spec(cols):
        return pl.BlockSpec((block, cols), lambda i: (i, 0))

    widths = (left, 2 * right)
    return pl.pallas_call(
        pack_kernel,
        grid=(rows // block,),
        in_specs=[spec(left), spec(width), spec(width)],
        out_specs=[spec(cols) for cols in widths],
        out_shape=[jax.ShapeDtypeStruct((rows, cols), BF16) for cols in widths],
        compiler_params=PARAMS,
        cost_estimate=cost(0, 8 * rows * width),
        name="pack_travellers",
    )(attn_query, attn_key, attn_value)


def move_kernel(sums, w_ref, m_ref, *refs):
    addends = refs[:sums]
    nw_ref, nm_ref, low_ref = refs[-3:]
    update = addends[0][...]
    for addend in addends[1:]:
        update = update + addend[...].astype(F32)
    weights = w_ref[...]
    momentum = DECAY * m_ref[...] + update
    moved = weights + momentum
    nm_ref[...] = momentum
    for part in range(3):
        cols = slice(part * FD, (part + 1) * FD)
        before = jnp.mean(jnp.square(weights[:, cols]), axis=1, keepdims=True)
        after = jnp.mean(jnp.square(moved[:, cols]), axis=1, keepdims=True)
        fresh = moved[:, cols] * (jnp.sqrt(before + EPSILON) * lax.rsqrt(after + EPSILON))
        nw_ref[:, cols] = fresh
        low_ref[:, cols] = fresh.astype(BF16)


def move_weights(fast_weights, momentum, addends, head, previous):
    rows = fast_weights.shape[0]
    block = row_block(rows, 80)
    wide = pl.BlockSpec((block, SPAN), lambda i: (i, head))
    own = pl.BlockSpec((block, SPAN), lambda i: (i, 0))
    in_specs = [wide, wide] + [own] * len(addends)
    args = [fast_weights, momentum] + list(addends)
    aliases = {}
    if previous is not None:
        aliases = {len(args): 0, len(args) + 1: 1}
        in_specs += [ANY, ANY]
        args += list(previous)
    full = jax.ShapeDtypeStruct(fast_weights.shape, F32)
    return pl.pallas_call(
        functools.partial(move_kernel, len(addends)),
        grid=(rows // block,),
        in_specs=in_specs,
        out_specs=(wide, wide, own),
        out_shape=(full, full, jax.ShapeDtypeStruct((rows, SPAN), BF16)),
        input_output_aliases=aliases,
        compiler_params=PARAMS,
        cost_estimate=cost(20 * rows * SPAN, 26 * rows * SPAN),
        name="move_weights",
    )(*args)


def query_kernel(masks, q_hbm, head, *refs):
    count = len(masks)
    parts = refs[:count]
    out_hbm, q_ref, low, stage, sems = refs[-5:]
    mine = slice(head * FD, (head + 1) * FD)
    copies = Copies(sems)
    query_copy = copies.start(q_hbm.at[:, mine], q_ref)
    loads = [copies.part(parts, masks, low, third) for third in range(3)]
    tokens = q_ref.shape[0]
    block = min(256, tokens)
    sent = []
    for first in range(0, tokens, block):
        rows = slice(first, first + block)
        if first == 0:
            wait([query_copy] + loads[0])
        queries = q_ref[rows, :]
        gate = dot(queries, low[:, :FD], 1, 1) * INV_ROOT
        if first == 0:
            wait(loads[1])
        up = dot(queries, low[:, FD : 2 * FD], 1, 1) * INV_ROOT
        hidden = (gate * (1.0 / (1.0 + jnp.exp(-gate))) * up).astype(BF16)
        if first == 0:
            wait(loads[2])
        stage[rows, :] = (dot(hidden, low[:, 2 * FD :], 1, 1) * INV_ROOT).astype(BF16)
        sent.append(copies.start(stage.at[rows, :], out_hbm.at[rows, mine]))
    wait(sent)


def head_query(fw_query, gathered, head, previous):
    tokens = fw_query.shape[0]
    parts = [part for part, _ in gathered]
    masks = [mask for _, mask in gathered]
    args = [fw_query] + parts
    aliases = {}
    if previous is not None:
        aliases = {len(args): 0}
        args.append(previous)
    by_token = pltpu.VMEM((tokens, FD), BF16)
    return pl.pallas_call(
        lambda q_hbm, *refs: query_kernel(masks, q_hbm, head, *refs),
        in_specs=[ANY] * len(args),
        out_specs=ANY,
        out_shape=jax.ShapeDtypeStruct(fw_query.shape, BF16),
        scratch_shapes=[
            by_token,
            pltpu.VMEM((FD, SPAN), BF16),
            by_token,
            pltpu.SemaphoreType.DMA((1 + 3 * len(parts) + pl.cdiv(tokens, 256),)),
        ],
        input_output_aliases=aliases,
        compiler_params=PARAMS,
        cost_estimate=cost(6 * tokens * FD * FD, 4e6, tokens * FD),
        name="head_query",
    )(*args)


def swapped(array, mask):
    devices = lax.axis_size("ctx")
    return lax.ppermute(array, "ctx", [(i, i ^ mask) for i in range(devices)])


def shifted(array, by):
    devices = lax.axis_size("ctx")
    pairs = [(i, i + by) for i in range(devices) if 0 <= i + by < devices]
    return lax.ppermute(array, "ctx", pairs)


def after(array, *others):
    return lax.optimization_barrier((array,) + others)[0]


def gather_rows(shard, paired):
    if not paired:
        return [(lax.all_gather(shard, "ctx", axis=0, tiled=True), None)]
    across = swapped(shard, 2)
    beside = swapped(shard, 1)
    return [(shard, 0), (beside, 1), (across, 2), (swapped(across, 1), 3)]


def sum_rows(pieces, paired):
    if not paired:
        return [lax.psum_scatter(pieces[0], "ctx", scatter_dimension=0, tiled=True)], pieces[0]
    far, near, across, own = pieces
    far = swapped(far, 1)
    near = swapped(near, 1)
    total = add_rows(across, far)
    return [own, near, swapped(total, 2)], total


def per_device(
    attn_query, attn_key, attn_value, fw_query, fw_key, fw_value, fw_rate, fast_weights, momentum
):
    devices = lax.axis_size("ctx")
    head_local = fw_rate.shape[1]
    paired = devices == 4
    heads = range(head_local)
    all_heads = attn_query.shape[1] // HD
    moved = 2 * all_heads // 5
    stay = all_heads - moved
    half = stay // 2 if stay % 2 == 0 else stay
    halves = range(0, stay, half)

    low = round_head(fast_weights, 0)
    gathered = [gather_rows(low, paired)]
    started = gathered[0][2 if paired else 0][0]
    own = attention_call(
        own_kernel,
        stay,
        [after(attn_query, low), attn_key, attn_value],
        [0, 0, 0],
        [("t", 0), ("s", 0)],
        0.6,
        most=half,
    )
    before = own[1]
    for head in heads[1:]:
        low = round_head(after(fast_weights, before), head)
        before = low
        gathered.append(gather_rows(after(low, started), paired))
    queries, pairs = pack_travellers(after(attn_query, before), attn_key, attn_value, stay)
    far_query = shifted(after(queries, started), -2)
    far_pairs = shifted(after(pairs, started), 2)
    far_pairs_other = swapped(far_pairs, 1)
    pair_key = swapped(attn_key, 1)
    pair_value = swapped(attn_value, 1)

    before = queries
    sums = []
    totals = []
    for head in heads:
        pieces = head_grads(after(fw_key, before), fw_value, fw_rate, gathered[head], head, paired)
        before = pieces[-1]
        addends, total = sum_rows(pieces, paired)
        sums.append(addends)
        totals.append(total)
    found = []
    for first in halves:
        found.append(
            attention_call(
                group_kernel,
                half,
                [
                    attn_query,
                    after(far_query, before),
                    attn_key,
                    attn_value,
                    pair_key,
                    pair_value,
                    *own,
                ],
                [first] * 6 + [("t", first), ("s", first)],
                [("f", 0), ("t", 0), ("s", 0)],
                1.6,
                most=half,
            )
        )
        before = after(found[-1][2], totals[-1])

    fw_new = None
    new_gathered = []
    for head in heads:
        new_weights, new_momentum, low = move_weights(
            fast_weights, momentum, sums[head], head, fw_new
        )
        fw_new = (new_weights, new_momentum)
        new_gathered.append(gather_rows(low, paired))
        if head == 0:
            attn_out = attention_call(
                whole_kernel,
                moved,
                [
                    after(attn_query, low),
                    attn_key,
                    attn_value,
                    pair_key,
                    pair_value,
                    far_pairs,
                    far_pairs,
                    far_pairs_other,
                    far_pairs_other,
                ],
                [stay] * 5 + [0, moved, 0, moved],
                [stay],
                2.2,
                (attn_query.shape, None),
                most=2,
            )[0]
            momentum = after(momentum, attn_out)
    returned = []
    for number, (far_o, own_o, own_st) in enumerate(found):
        if number > 0:
            far_o = after(far_o, low)
        returned.append((own_o, own_st, shifted(far_o, 2)))
    fw_out = None
    for head in heads:
        fw_out = head_query(fw_query, new_gathered[head], head, fw_out)
    for number, states in enumerate(returned):
        attn_out = attention_call(
            merge_kernel,
            half,
            states,
            [("t", 0), ("s", 0), ("f", 0)],
            [number * half],
            0.01,
            (attn_query.shape, attn_out),
            most=half,
        )[0]
    return (attn_out, fw_out, new_weights, new_momentum)


def solution(mesh):
    spec = P(("seq", "ctx"), "head")

    return jax.shard_map(
        per_device, mesh=mesh, in_specs=(spec,) * 9, out_specs=(spec,) * 4, check_vma=False
    )
```

```python
import functools
import math

import jax
import jax.numpy as jnp
from jax import lax
from jax.experimental import pallas as pl
from jax.experimental.pallas import tpu as pltpu
from jax.sharding import PartitionSpec as P


HD = 128
FD = 640
EPSILON = 1e-06
DECAY = 0.9
SPAN = 3 * FD
INV_ROOT = FD ** (-0.5)
EXP2_SCALE = HD ** (-0.5) * math.log2(math.e)
LOWEST = -1e30
F32 = jnp.float32
BF16 = jnp.bfloat16
ANY = pl.BlockSpec(memory_space=pltpu.HBM)
PARAMS = pltpu.CompilerParams(vmem_limit_bytes=67043328)


def dot(a, b, a_dim, b_dim):
    return lax.dot_general(a, b, (((a_dim,), (b_dim,)), ((), ())), preferred_element_type=F32)


def cost(flops, bytes_accessed, transcendentals=0):
    return pl.CostEstimate(
        flops=int(flops), bytes_accessed=int(bytes_accessed), transcendentals=int(transcendentals)
    )


CHUNK = 128


def soft(scores, values):
    highest = jnp.max(scores, axis=0, keepdims=True)
    weights = jnp.exp2((scores - highest) * EXP2_SCALE)
    total = jnp.sum(weights, axis=0, keepdims=True)
    return dot(values, weights.astype(BF16), 0, 0), highest, total


def masked(scores, causal, first_key, first_query):
    key_row = lax.broadcasted_iota(jnp.int32, scores.shape, 0) + first_key
    query_row = lax.broadcasted_iota(jnp.int32, scores.shape, 1) + first_query
    allowed = key_row <= query_row if causal else key_row > query_row
    return jnp.where(allowed, scores, LOWEST)


def scaled_to(before, after):
    return jnp.exp2((before - after) * EXP2_SCALE)


def own_kernel(per_step, q_ref, k_ref, v_ref, o_ref, st_ref):
    for g in range(per_step):
        cols = slice(g * HD, (g + 1) * HD)
        for first in range(0, q_ref.shape[0], CHUNK):
            rows = slice(first, first + CHUNK)
            upto = first + CHUNK
            scores = masked(dot(k_ref[:upto, cols], q_ref[rows, cols], 1, 1), True, 0, first)
            mixed, highest, total = soft(scores, v_ref[:upto, cols])
            o_ref[cols, rows] = mixed.astype(BF16)
            st_ref[g : g + 1, rows] = highest
            st_ref[per_step + g : per_step + g + 1, rows] = total


def pieces_of(value, count):
    rows = []
    for _ in range(count):
        rows.append(value.astype(BF16).astype(F32))
        value = value - rows[-1]
    return rows


def stat_places(per_step):
    return 16 * pl.cdiv(5 * per_step, 16)


def group_kernel(
    per_step, q_ref, far_ref, k_ref, v_ref, pk_ref, pv_ref, o_ref, st_ref, fo_ref, lo_ref, lst_ref
):
    leading = lax.axis_index("ctx") % 2 == 0
    places = stat_places(per_step)
    for first in range(0, q_ref.shape[0], CHUNK):
        rows = slice(first, first + CHUNK)
        stats = []
        for g in range(per_step):
            cols = slice(g * HD, (g + 1) * HD)
            top, bottom = slice(g, g + 1), slice(per_step + g, per_step + g + 1)
            far = far_ref[rows, cols]
            scores = masked(dot(k_ref[first:, cols], far, 1, 1), False, first, first)
            far_o, far_m, far_l = soft(scores, v_ref[first:, cols])
            guest = jnp.where(leading, far, q_ref[rows, cols])
            mixed, highest, total = soft(dot(pk_ref[:, cols], guest, 1, 1), pv_ref[:, cols])
            far_top = jnp.where(leading, jnp.maximum(far_m, highest), far_m)
            far_keep = scaled_to(far_m, far_top)
            far_add = jnp.where(leading, scaled_to(highest, far_top), 0.0)
            fo_ref[cols, rows] = (far_o * far_keep + mixed * far_add).astype(BF16)
            stats += pieces_of(far_top, 3) + pieces_of(far_l * far_keep + total * far_add, 2)
            own_m = st_ref[top, rows]
            own_top = jnp.where(leading, own_m, jnp.maximum(own_m, highest))
            own_keep = scaled_to(own_m, own_top)
            own_add = jnp.where(leading, 0.0, scaled_to(highest, own_top))
            lo_ref[cols, rows] = (o_ref[cols, rows].astype(F32) * own_keep + mixed * own_add).astype(BF16)
            lst_ref[top, rows] = own_top
            lst_ref[bottom, rows] = st_ref[bottom, rows] * own_keep + total * own_add
        stats += [jnp.zeros_like(stats[0])] * (places - len(stats))
        fo_ref[per_step * HD :, rows] = jnp.concatenate(stats, axis=0).astype(BF16)


def merge_kernel(per_step, o_ref, st_ref, fo_ref, out_ref):
    valid = lax.axis_index("ctx") >= 2
    stats = fo_ref[per_step * HD :, :].astype(F32)
    for g in range(per_step):
        cols = slice(g * HD, (g + 1) * HD)
        top, bottom = slice(g, g + 1), slice(per_step + g, per_step + g + 1)
        m0, m1, m2, l0, l1 = [stats[5 * g + i : 5 * g + i + 1, :] for i in range(5)]
        own_m = st_ref[top, :]
        far_m = jnp.where(valid, m0 + m1 + m2, LOWEST)
        highest = jnp.maximum(own_m, far_m)
        own_keep = scaled_to(own_m, highest)
        far_keep = scaled_to(far_m, highest)
        total = st_ref[bottom, :] * own_keep + (l0 + l1) * far_keep
        mixed = o_ref[cols, :].astype(F32) * own_keep + fo_ref[cols, :].astype(F32) * far_keep
        out_ref[:, cols] = (mixed / total).T.astype(BF16)


def whole_kernel(
    per_step, q_ref, k_ref, v_ref, pk_ref, pv_ref, fk_ref, fv_ref, fpk_ref, fpv_ref, out_ref
):
    index = lax.axis_index("ctx")
    leading = index % 2 == 0
    valid = index >= 2
    beside = jnp.logical_or(valid, jnp.logical_not(leading))
    for g in range(per_step):
        cols = slice(g * HD, (g + 1) * HD)
        other_k = jnp.where(leading, fpk_ref[:, cols], pk_ref[:, cols])
        other_v = jnp.where(leading, fpv_ref[:, cols], pv_ref[:, cols])
        for first in range(0, q_ref.shape[0], CHUNK):
            rows = slice(first, first + CHUNK)
            upto = first + CHUNK
            queries = q_ref[rows, cols]
            own = masked(dot(k_ref[:upto, cols], queries, 1, 1), True, 0, first)
            far = masked(dot(fk_ref[first:, cols], queries, 1, 1), False, first, first)
            own_o, own_m, own_l = soft(own, v_ref[:upto, cols])
            far_o, far_m, far_l = soft(far, fv_ref[first:, cols])
            other_o, other_m, other_l = soft(dot(other_k, queries, 1, 1), other_v)
            far_m = jnp.where(valid, far_m, LOWEST)
            other_m = jnp.where(beside, other_m, LOWEST)
            highest = jnp.maximum(jnp.maximum(own_m, far_m), other_m)
            own_f = scaled_to(own_m, highest)
            far_f = scaled_to(far_m, highest)
            other_f = scaled_to(other_m, highest)
            total = own_l * own_f + far_l * far_f + other_l * other_f
            mixed = own_o * own_f + far_o * far_f + other_o * other_f
            out_ref[rows, cols] = (mixed / total).T.astype(BF16)


def attention_call(kernel, heads, arrays, firsts, outs, units, into=None, most=5):
    firsts, outs = [[f if isinstance(f, tuple) else ("c", f) for f in fs] for fs in (firsts, outs)]
    rows = arrays[0].shape[firsts[0][0] != "c"]
    per_step = max(
        size
        for size in range(1, most + 1)
        if heads % size == 0 and all(f % size == 0 for _, f in firsts + outs)
    )

    stat_rows = 8 * pl.cdiv(2 * per_step, 8)
    far_rows = per_step * HD + stat_places(per_step)

    def spec(kind, first):
        step = first // per_step
        if kind == "t":
            return pl.BlockSpec((per_step * HD, rows), lambda i: (i + step, 0))
        if kind == "s":
            return pl.BlockSpec((stat_rows, rows), lambda i: (i + step, 0))
        if kind == "f":
            return pl.BlockSpec((far_rows, rows), lambda i: (i + step, 0))
        return pl.BlockSpec((rows, per_step * HD), lambda i: (0, i + step))

    def shape(kind):
        if kind == "t":
            return jax.ShapeDtypeStruct((heads * HD, rows), BF16)
        if kind == "f":
            return jax.ShapeDtypeStruct((far_rows * (heads // per_step), rows), BF16)
        if kind == "s":
            return jax.ShapeDtypeStruct((stat_rows * (heads // per_step), rows), F32)
        return jax.ShapeDtypeStruct(into[0], BF16)

    aliases = {}
    in_specs = [spec(*first) for first in firsts]
    body = functools.partial(kernel, per_step)
    if into is not None and into[1] is not None:
        aliases = {len(arrays): 0}
        count = len(arrays)
        arrays = list(arrays) + [into[1]]
        in_specs.append(ANY)
        inner = body
        body = lambda *refs: inner(*refs[:count], *refs[count + 1 :])
    return pl.pallas_call(
        body,
        grid=(heads // per_step,),
        in_specs=in_specs,
        out_specs=[spec(*first) for first in outs],
        out_shape=[shape(kind) for kind, _ in outs],
        input_output_aliases=aliases,
        compiler_params=PARAMS,
        cost_estimate=cost(
            4 * units * rows * rows * heads * HD,
            len(firsts + outs) * rows * heads * HD * 2,
            units * rows * rows * heads,
        ),
    )(*arrays)


def rows_of(mask, rows):
    return pl.ds(pl.multiple_of((lax.axis_index("ctx") ^ mask) * rows, 32), rows)


class Copies:
    def __init__(self, sems):
        self.sems = sems
        self.used = 0

    def start(self, source, target):
        copy = pltpu.make_async_copy(source, target, self.sems.at[self.used])
        self.used += 1
        copy.start()
        return copy

    def part(self, parts, masks, low, third):
        cols = slice(third * FD, (third + 1) * FD)
        copies = []
        for part, mask in zip(parts, masks):
            rows = part.shape[0]
            place = slice(None) if mask is None else rows_of(mask, rows)
            copies.append(self.start(part.at[:, cols], low.at[place, cols]))
        return copies


def wait(copies):
    for copy in copies:
        copy.wait()


def grads_kernel(masks, split, head, *refs):
    count = len(masks)
    rate_ref, key_hbm, value_hbm = refs[:3]
    parts = refs[3 : 3 + count]
    outs = refs[3 + count : -10]
    key_ref, value_ref, low, scaled, hidden, gate_grad, up_grad, update, stage, sems = refs[-10:]
    mine = slice(head * FD, (head + 1) * FD)
    copies = Copies(sems)
    key_copy = copies.start(key_hbm.at[:, mine], key_ref)
    gate_copies = copies.part(parts, masks, low, 0)
    up_copies = copies.part(parts, masks, low, 1)
    value_copy = copies.start(value_hbm.at[:, mine], value_ref)
    back_copies = copies.part(parts, masks, low, 2)
    tokens = key_ref.shape[0]
    rate = jnp.broadcast_to(rate_ref[head : head + 1, :], (8, tokens)).T[:, :1]
    block = min(256, tokens)
    for first in range(0, tokens, block):
        rows = slice(first, first + block)
        if first == 0:
            wait([key_copy] + gate_copies)
        keys = key_ref[rows, :]
        gate = dot(keys, low[:, :FD], 1, 1) * INV_ROOT
        if first == 0:
            wait(up_copies)
        up = dot(keys, low[:, FD : 2 * FD], 1, 1) * INV_ROOT
        if first == 0:
            wait([value_copy])
            scaled[...] = (rate * value_ref[...].astype(F32)).astype(BF16)
            wait(back_copies)
        back = dot(scaled[rows, :], low[:, 2 * FD :], 1, 0) * INV_ROOT
        sigmoid = 1.0 / (1.0 + jnp.exp(-gate))
        silu = gate * sigmoid
        hidden[rows, :] = (silu * up).astype(BF16)
        gate_grad[rows, :] = (back * up * sigmoid * (1.0 + gate * (1.0 - sigmoid))).astype(BF16)
        up_grad[rows, :] = (back * silu).astype(BF16)
    sent = []
    for third, (left, right) in enumerate(((gate_grad, key_ref), (up_grad, key_ref), (scaled, hidden))):
        cols = slice(third * FD, (third + 1) * FD)
        for first in range(0, FD, 128):
            rows = slice(first, first + 128)
            update[rows, cols] = dot(left[:, rows], right[...], 0, 0)
        if split:
            far, near, across, own = outs
            rows = far.shape[0]
            for number, (out, mask) in enumerate(((far, 3), (near, 1), (across, 2))):
                place = slice(number * rows, (number + 1) * rows)
                stage[place, cols] = update[rows_of(mask, rows), cols].astype(BF16)
                sent.append(copies.start(stage.at[place, cols], out.at[:, cols]))
            sent.append(copies.start(update.at[rows_of(0, rows), cols], own.at[:, cols]))
        else:
            sent.append(copies.start(update.at[:, cols], outs[0].at[:, cols]))
    wait(sent)


def head_grads(fw_key, fw_value, fw_rate, gathered, head, split):
    tokens = fw_key.shape[0]
    parts = [part for part, _ in gathered]
    masks = [mask for _, mask in gathered]
    if split:
        rows = parts[0].shape[0]
        out_shape = tuple(jax.ShapeDtypeStruct((rows, SPAN), kind) for kind in (BF16, BF16, BF16, F32))
    else:
        out_shape = (jax.ShapeDtypeStruct((FD, SPAN), F32),)
    by_token = pltpu.VMEM((tokens, FD), BF16)
    return pl.pallas_call(
        functools.partial(grads_kernel, masks, split, head),
        in_specs=[pl.BlockSpec(memory_space=pltpu.VMEM)] + [ANY] * (2 + len(parts)),
        out_specs=tuple(ANY for _ in out_shape),
        out_shape=out_shape,
        scratch_shapes=[
            by_token,
            by_token,
            pltpu.VMEM((FD, SPAN), BF16),
            by_token,
            by_token,
            by_token,
            by_token,
            pltpu.VMEM((FD, SPAN), F32),
            pltpu.VMEM((3 * parts[0].shape[0] if split else 16, SPAN), BF16),
            pltpu.SemaphoreType.DMA((2 + 3 * len(parts) + 3 * len(out_shape),)),
        ],
        compiler_params=PARAMS,
        cost_estimate=cost(12 * tokens * FD * FD, 8e6, tokens * FD),
        name="head_grads",
    )(fw_rate.T, fw_key, fw_value, *parts)


def add_kernel(left_ref, right_ref, sum_ref):
    sum_ref[...] = (left_ref[...].astype(F32) + right_ref[...].astype(F32)).astype(BF16)


def add_rows(left, right):
    rows, width = left.shape
    block = row_block(rows, 80)
    spec = pl.BlockSpec((block, width), lambda i: (i, 0))
    return pl.pallas_call(
        add_kernel,
        grid=(rows // block,),
        in_specs=[spec, spec],
        out_specs=spec,
        out_shape=jax.ShapeDtypeStruct((rows, width), BF16),
        compiler_params=PARAMS,
        cost_estimate=cost(rows * width, 6 * rows * width),
        name="add_rows",
    )(left, right)


def round_kernel(w_ref, low_ref):
    low_ref[...] = w_ref[...].astype(BF16)


def row_block(rows, most):
    return max((size for size in range(16, most + 1, 16) if rows % size == 0), default=rows)


def round_head(fast_weights, head):
    rows = fast_weights.shape[0]
    block = row_block(rows, 80)
    return pl.pallas_call(
        round_kernel,
        grid=(rows // block,),
        in_specs=[pl.BlockSpec((block, SPAN), lambda i: (i, head))],
        out_specs=pl.BlockSpec((block, SPAN), lambda i: (i, 0)),
        out_shape=jax.ShapeDtypeStruct((rows, SPAN), BF16),
        compiler_params=PARAMS,
        cost_estimate=cost(rows * SPAN, 6 * rows * SPAN),
        name="round_head",
    )(fast_weights)


def pack_kernel(q_ref, k_ref, v_ref, queries_ref, pairs_ref):
    first, width = queries_ref.shape[1], pairs_ref.shape[1] // 2
    queries_ref[...] = q_ref[...]
    pairs_ref[:, :width] = k_ref[:, first:]
    pairs_ref[:, width:] = v_ref[:, first:]


def pack_travellers(attn_query, attn_key, attn_value, stay):
    rows, width = attn_query.shape
    block = row_block(rows, 256)
    left, right = stay * HD, width - stay * HD

    def spec(cols):
        return pl.BlockSpec((block, cols), lambda i: (i, 0))

    widths = (left, 2 * right)
    return pl.pallas_call(
        pack_kernel,
        grid=(rows // block,),
        in_specs=[spec(left), spec(width), spec(width)],
        out_specs=[spec(cols) for cols in widths],
        out_shape=[jax.ShapeDtypeStruct((rows, cols), BF16) for cols in widths],
        compiler_params=PARAMS,
        cost_estimate=cost(0, 8 * rows * width),
        name="pack_travellers",
    )(attn_query, attn_key, attn_value)


def move_kernel(sums, w_ref, m_ref, *refs):
    addends = refs[:sums]
    nw_ref, nm_ref, low_ref = refs[-3:]
    update = addends[0][...]
    for addend in addends[1:]:
        update = update + addend[...].astype(F32)
    weights = w_ref[...]
    momentum = DECAY * m_ref[...] + update
    moved = weights + momentum
    nm_ref[...] = momentum
    for part in range(3):
        cols = slice(part * FD, (part + 1) * FD)
        before = jnp.mean(jnp.square(weights[:, cols]), axis=1, keepdims=True)
        after = jnp.mean(jnp.square(moved[:, cols]), axis=1, keepdims=True)
        fresh = moved[:, cols] * (jnp.sqrt(before + EPSILON) * lax.rsqrt(after + EPSILON))
        nw_ref[:, cols] = fresh
        low_ref[:, cols] = fresh.astype(BF16)


def move_weights(fast_weights, momentum, addends, head, previous):
    rows = fast_weights.shape[0]
    block = row_block(rows, 80)
    wide = pl.BlockSpec((block, SPAN), lambda i: (i, head))
    own = pl.BlockSpec((block, SPAN), lambda i: (i, 0))
    in_specs = [wide, wide] + [own] * len(addends)
    args = [fast_weights, momentum] + list(addends)
    aliases = {}
    if previous is not None:
        aliases = {len(args): 0, len(args) + 1: 1}
        in_specs += [ANY, ANY]
        args += list(previous)
    full = jax.ShapeDtypeStruct(fast_weights.shape, F32)
    return pl.pallas_call(
        functools.partial(move_kernel, len(addends)),
        grid=(rows // block,),
        in_specs=in_specs,
        out_specs=(wide, wide, own),
        out_shape=(full, full, jax.ShapeDtypeStruct((rows, SPAN), BF16)),
        input_output_aliases=aliases,
        compiler_params=PARAMS,
        cost_estimate=cost(20 * rows * SPAN, 26 * rows * SPAN),
        name="move_weights",
    )(*args)


def query_kernel(masks, q_hbm, head, *refs):
    count = len(masks)
    parts = refs[:count]
    out_hbm, q_ref, low, stage, sems = refs[-5:]
    mine = slice(head * FD, (head + 1) * FD)
    copies = Copies(sems)
    query_copy = copies.start(q_hbm.at[:, mine], q_ref)
    loads = [copies.part(parts, masks, low, third) for third in range(3)]
    tokens = q_ref.shape[0]
    block = min(256, tokens)
    sent = []
    for first in range(0, tokens, block):
        rows = slice(first, first + block)
        if first == 0:
            wait([query_copy] + loads[0])
        queries = q_ref[rows, :]
        gate = dot(queries, low[:, :FD], 1, 1) * INV_ROOT
        if first == 0:
            wait(loads[1])
        up = dot(queries, low[:, FD : 2 * FD], 1, 1) * INV_ROOT
        hidden = (gate * (1.0 / (1.0 + jnp.exp(-gate))) * up).astype(BF16)
        if first == 0:
            wait(loads[2])
        stage[rows, :] = (dot(hidden, low[:, 2 * FD :], 1, 1) * INV_ROOT).astype(BF16)
        sent.append(copies.start(stage.at[rows, :], out_hbm.at[rows, mine]))
    wait(sent)


def head_query(fw_query, gathered, head, previous):
    tokens = fw_query.shape[0]
    parts = [part for part, _ in gathered]
    masks = [mask for _, mask in gathered]
    args = [fw_query] + parts
    aliases = {}
    if previous is not None:
        aliases = {len(args): 0}
        args.append(previous)
    by_token = pltpu.VMEM((tokens, FD), BF16)
    return pl.pallas_call(
        lambda q_hbm, *refs: query_kernel(masks, q_hbm, head, *refs),
        in_specs=[ANY] * len(args),
        out_specs=ANY,
        out_shape=jax.ShapeDtypeStruct(fw_query.shape, BF16),
        scratch_shapes=[
            by_token,
            pltpu.VMEM((FD, SPAN), BF16),
            by_token,
            pltpu.SemaphoreType.DMA((1 + 3 * len(parts) + pl.cdiv(tokens, 256),)),
        ],
        input_output_aliases=aliases,
        compiler_params=PARAMS,
        cost_estimate=cost(6 * tokens * FD * FD, 4e6, tokens * FD),
        name="head_query",
    )(*args)


def swapped(array, mask):
    devices = lax.axis_size("ctx")
    return lax.ppermute(array, "ctx", [(i, i ^ mask) for i in range(devices)])


def shifted(array, by):
    devices = lax.axis_size("ctx")
    pairs = [(i, i + by) for i in range(devices) if 0 <= i + by < devices]
    return lax.ppermute(array, "ctx", pairs)


def after(array, *others):
    return lax.optimization_barrier((array,) + others)[0]


def gather_rows(shard, paired):
    if not paired:
        return [(lax.all_gather(shard, "ctx", axis=0, tiled=True), None)]
    across = swapped(shard, 2)
    beside = swapped(shard, 1)
    return [(shard, 0), (beside, 1), (across, 2), (swapped(across, 1), 3)]


def sum_rows(pieces, paired):
    if not paired:
        return [lax.psum_scatter(pieces[0], "ctx", scatter_dimension=0, tiled=True)], pieces[0]
    far, near, across, own = pieces
    far = swapped(far, 1)
    near = swapped(near, 1)
    total = add_rows(across, far)
    return [own, near, swapped(total, 2)], total


def per_device(
    attn_query, attn_key, attn_value, fw_query, fw_key, fw_value, fw_rate, fast_weights, momentum
):
    devices = lax.axis_size("ctx")
    head_local = fw_rate.shape[1]
    paired = devices == 4
    heads = range(head_local)
    all_heads = attn_query.shape[1] // HD
    moved = all_heads // 5
    stay = all_heads - moved
    half = stay // 2 if stay % 2 == 0 else stay
    halves = range(0, stay, half)

    low = round_head(fast_weights, 0)
    gathered = [gather_rows(low, paired)]
    started = gathered[0][2 if paired else 0][0]
    own = attention_call(
        own_kernel,
        stay,
        [after(attn_query, low), attn_key, attn_value],
        [0, 0, 0],
        [("t", 0), ("s", 0)],
        0.6,
        most=half,
    )
    before = own[1]
    for head in heads[1:]:
        low = round_head(after(fast_weights, before), head)
        before = low
        gathered.append(gather_rows(after(low, started), paired))
    queries, pairs = pack_travellers(after(attn_query, before), attn_key, attn_value, stay)
    far_query = shifted(after(queries, started), -2)
    far_pairs = shifted(after(pairs, started), 2)
    far_pairs_other = swapped(far_pairs, 1)
    pair_key = swapped(attn_key, 1)
    pair_value = swapped(attn_value, 1)

    before = queries
    sums = []
    totals = []
    for head in heads:
        pieces = head_grads(after(fw_key, before), fw_value, fw_rate, gathered[head], head, paired)
        before = pieces[-1]
        addends, total = sum_rows(pieces, paired)
        sums.append(addends)
        totals.append(total)
    before = totals[-1]
    fw_new = None
    new_gathered = []
    found = []
    for number in range(max(len(halves), head_local)):
        if number < len(halves):
            first = halves[number]
            far_o, own_o, own_st = attention_call(
                group_kernel,
                half,
                [
                    attn_query,
                    after(far_query, before),
                    attn_key,
                    attn_value,
                    pair_key,
                    pair_value,
                    *own,
                ],
                [first] * 6 + [("t", first), ("s", first)],
                [("f", 0), ("t", 0), ("s", 0)],
                1.6,
                most=half,
            )
            found.append((far_o, own_o, own_st))
            before = own_st
        if number < head_local:
            new_weights, new_momentum, low = move_weights(
                fast_weights, after(momentum, before), sums[number], number, fw_new
            )
            fw_new = (new_weights, new_momentum)
            new_gathered.append(gather_rows(low, paired))
            before = low
    attn_out = attention_call(
        whole_kernel,
        moved,
        [
            after(attn_query, before),
            attn_key,
            attn_value,
            pair_key,
            pair_value,
            far_pairs,
            far_pairs,
            far_pairs_other,
            far_pairs_other,
        ],
        [stay] * 5 + [0, moved, 0, moved],
        [stay],
        2.2,
        (attn_query.shape, None),
        most=2,
    )[0]
    returned = []
    for number, (far_o, own_o, own_st) in enumerate(found):
        if number > 0:
            far_o = after(far_o, low)
        returned.append((own_o, own_st, shifted(far_o, 2)))
    fw_out = None
    for head in heads:
        fw_out = head_query(fw_query, new_gathered[head], head, fw_out)
    for number, states in enumerate(returned):
        attn_out = attention_call(
            merge_kernel,
            half,
            states,
            [("t", 0), ("s", 0), ("f", 0)],
            [number * half],
            0.01,
            (attn_query.shape, attn_out),
            most=half,
        )[0]
    return (attn_out, fw_out, new_weights, new_momentum)


def solution(mesh):
    spec = P(("seq", "ctx"), "head")

    return jax.shard_map(
        per_device, mesh=mesh, in_specs=(spec,) * 9, out_specs=(spec,) * 4, check_vma=False
    )
```

```python
import functools
import math

import jax
import jax.numpy as jnp
from jax import lax
from jax.experimental import pallas as pl
from jax.experimental.pallas import tpu as pltpu
from jax.sharding import PartitionSpec as P


HD = 128
FD = 640
EPSILON = 1e-06
DECAY = 0.9
SPAN = 3 * FD
INV_ROOT = FD ** (-0.5)
EXP2_SCALE = HD ** (-0.5) * math.log2(math.e)
LOWEST = -(2.0**100)
F32 = jnp.float32
BF16 = jnp.bfloat16
ANY = pl.BlockSpec(memory_space=pltpu.HBM)
PARAMS = pltpu.CompilerParams(vmem_limit_bytes=67043328)


def dot(a, b, a_dim, b_dim):
    return lax.dot_general(a, b, (((a_dim,), (b_dim,)), ((), ())), preferred_element_type=F32)


def cost(flops, bytes_accessed, transcendentals=0):
    return pl.CostEstimate(
        flops=int(flops), bytes_accessed=int(bytes_accessed), transcendentals=int(transcendentals)
    )


CHUNK = 128


def soft(scores, values):
    highest = jnp.max(scores, axis=0, keepdims=True)
    weights = jnp.exp2((scores - highest) * EXP2_SCALE)
    total = jnp.sum(weights, axis=0, keepdims=True)
    return dot(values, weights.astype(BF16), 0, 0), highest, total


def masked(scores, causal, first_key, first_query):
    key_row = lax.broadcasted_iota(jnp.int32, scores.shape, 0) + first_key
    query_row = lax.broadcasted_iota(jnp.int32, scores.shape, 1) + first_query
    allowed = key_row <= query_row if causal else key_row > query_row
    return jnp.where(allowed, scores, LOWEST)


def scaled_to(before, after):
    return jnp.exp2((before - after) * EXP2_SCALE)


def own_kernel(per_step, q_ref, k_ref, v_ref, o_ref, st_ref):
    for g in range(per_step):
        cols = slice(g * HD, (g + 1) * HD)
        for first in range(0, q_ref.shape[0], CHUNK):
            rows = slice(first, first + CHUNK)
            upto = first + CHUNK
            scores = masked(dot(k_ref[:upto, cols], q_ref[rows, cols], 1, 1), True, 0, first)
            mixed, highest, total = soft(scores, v_ref[:upto, cols])
            o_ref[cols, rows] = mixed.astype(BF16)
            st_ref[g : g + 1, rows] = highest
            st_ref[per_step + g : per_step + g + 1, rows] = total


def pieces_of(value, count):
    rows = []
    for _ in range(count):
        rows.append(value.astype(BF16).astype(F32))
        value = value - rows[-1]
    return rows


def stat_places(per_step):
    return 16 * pl.cdiv(4 * per_step, 16)


def group_kernel(
    per_step, q_ref, far_ref, k_ref, v_ref, pk_ref, pv_ref, o_ref, st_ref, fo_ref, lo_ref, lst_ref
):
    leading = lax.axis_index("ctx") % 2 == 0
    places = stat_places(per_step)
    for first in range(0, q_ref.shape[0], CHUNK):
        rows = slice(first, first + CHUNK)
        stats = []
        for g in range(per_step):
            cols = slice(g * HD, (g + 1) * HD)
            top, bottom = slice(g, g + 1), slice(per_step + g, per_step + g + 1)
            far = far_ref[rows, cols]
            scores = masked(dot(k_ref[first:, cols], far, 1, 1), False, first, first)
            far_o, far_m, far_l = soft(scores, v_ref[first:, cols])
            guest = jnp.where(leading, far, q_ref[rows, cols])
            mixed, highest, total = soft(dot(pk_ref[:, cols], guest, 1, 1), pv_ref[:, cols])
            far_top = jnp.where(leading, jnp.maximum(far_m, highest), far_m)
            top_rows = pieces_of(far_top, 2)
            far_top = top_rows[0] + top_rows[1]
            far_keep = scaled_to(far_m, far_top)
            far_add = jnp.where(leading, scaled_to(highest, far_top), 0.0)
            fo_ref[cols, rows] = (far_o * far_keep + mixed * far_add).astype(BF16)
            stats += top_rows + pieces_of(far_l * far_keep + total * far_add, 2)
            own_m = st_ref[top, rows]
            own_top = jnp.where(leading, own_m, jnp.maximum(own_m, highest))
            own_keep = scaled_to(own_m, own_top)
            own_add = jnp.where(leading, 0.0, scaled_to(highest, own_top))
            lo_ref[cols, rows] = (o_ref[cols, rows].astype(F32) * own_keep + mixed * own_add).astype(BF16)
            lst_ref[top, rows] = own_top
            lst_ref[bottom, rows] = st_ref[bottom, rows] * own_keep + total * own_add
        stats += [jnp.zeros_like(stats[0])] * (places - len(stats))
        fo_ref[per_step * HD :, rows] = jnp.concatenate(stats, axis=0).astype(BF16)


def merge_kernel(per_step, o_ref, st_ref, fo_ref, out_ref):
    valid = lax.axis_index("ctx") >= 2
    stats = fo_ref[per_step * HD :, :].astype(F32)
    for g in range(per_step):
        cols = slice(g * HD, (g + 1) * HD)
        top, bottom = slice(g, g + 1), slice(per_step + g, per_step + g + 1)
        m0, m1, l0, l1 = [stats[4 * g + i : 4 * g + i + 1, :] for i in range(4)]
        own_m = st_ref[top, :]
        far_m = jnp.where(valid, m0 + m1, LOWEST)
        highest = jnp.maximum(own_m, far_m)
        own_keep = scaled_to(own_m, highest)
        far_keep = scaled_to(far_m, highest)
        total = st_ref[bottom, :] * own_keep + (l0 + l1) * far_keep
        mixed = o_ref[cols, :].astype(F32) * own_keep + fo_ref[cols, :].astype(F32) * far_keep
        out_ref[:, cols] = (mixed / total).T.astype(BF16)


def whole_kernel(
    per_step, q_ref, k_ref, v_ref, pk_ref, pv_ref, fk_ref, fv_ref, fpk_ref, fpv_ref, out_ref
):
    index = lax.axis_index("ctx")
    leading = index % 2 == 0
    valid = index >= 2
    beside = jnp.logical_or(valid, jnp.logical_not(leading))
    for g in range(per_step):
        cols = slice(g * HD, (g + 1) * HD)
        other_k = jnp.where(leading, fpk_ref[:, cols], pk_ref[:, cols])
        other_v = jnp.where(leading, fpv_ref[:, cols], pv_ref[:, cols])
        for first in range(0, q_ref.shape[0], CHUNK):
            rows = slice(first, first + CHUNK)
            upto = first + CHUNK
            queries = q_ref[rows, cols]
            own = masked(dot(k_ref[:upto, cols], queries, 1, 1), True, 0, first)
            far = masked(dot(fk_ref[first:, cols], queries, 1, 1), False, first, first)
            own_o, own_m, own_l = soft(own, v_ref[:upto, cols])
            far_o, far_m, far_l = soft(far, fv_ref[first:, cols])
            other_o, other_m, other_l = soft(dot(other_k, queries, 1, 1), other_v)
            far_m = jnp.where(valid, far_m, LOWEST)
            other_m = jnp.where(beside, other_m, LOWEST)
            highest = jnp.maximum(jnp.maximum(own_m, far_m), other_m)
            own_f = scaled_to(own_m, highest)
            far_f = scaled_to(far_m, highest)
            other_f = scaled_to(other_m, highest)
            total = own_l * own_f + far_l * far_f + other_l * other_f
            mixed = own_o * own_f + far_o * far_f + other_o * other_f
            out_ref[rows, cols] = (mixed / total).T.astype(BF16)


def attention_call(kernel, heads, arrays, firsts, outs, units, into=None, most=5):
    firsts, outs = [[f if isinstance(f, tuple) else ("c", f) for f in fs] for fs in (firsts, outs)]
    rows = arrays[0].shape[firsts[0][0] != "c"]
    per_step = max(
        size
        for size in range(1, most + 1)
        if heads % size == 0 and all(f % size == 0 for _, f in firsts + outs)
    )

    stat_rows = 8 * pl.cdiv(2 * per_step, 8)
    far_rows = per_step * HD + stat_places(per_step)

    def spec(kind, first):
        step = first // per_step
        if kind == "t":
            return pl.BlockSpec((per_step * HD, rows), lambda i: (i + step, 0))
        if kind == "s":
            return pl.BlockSpec((stat_rows, rows), lambda i: (i + step, 0))
        if kind == "f":
            return pl.BlockSpec((far_rows, rows), lambda i: (i + step, 0))
        return pl.BlockSpec((rows, per_step * HD), lambda i: (0, i + step))

    def shape(kind):
        if kind == "t":
            return jax.ShapeDtypeStruct((heads * HD, rows), BF16)
        if kind == "f":
            return jax.ShapeDtypeStruct((far_rows * (heads // per_step), rows), BF16)
        if kind == "s":
            return jax.ShapeDtypeStruct((stat_rows * (heads // per_step), rows), F32)
        return jax.ShapeDtypeStruct(into[0], BF16)

    aliases = {}
    in_specs = [spec(*first) for first in firsts]
    body = functools.partial(kernel, per_step)
    if into is not None and into[1] is not None:
        aliases = {len(arrays): 0}
        count = len(arrays)
        arrays = list(arrays) + [into[1]]
        in_specs.append(ANY)
        inner = body
        body = lambda *refs: inner(*refs[:count], *refs[count + 1 :])
    return pl.pallas_call(
        body,
        grid=(heads // per_step,),
        in_specs=in_specs,
        out_specs=[spec(*first) for first in outs],
        out_shape=[shape(kind) for kind, _ in outs],
        input_output_aliases=aliases,
        compiler_params=PARAMS,
        cost_estimate=cost(
            4 * units * rows * rows * heads * HD,
            len(firsts + outs) * rows * heads * HD * 2,
            units * rows * rows * heads,
        ),
    )(*arrays)


def rows_of(mask, rows):
    return pl.ds(pl.multiple_of((lax.axis_index("ctx") ^ mask) * rows, 32), rows)


class Copies:
    def __init__(self, sems):
        self.sems = sems
        self.used = 0

    def start(self, source, target):
        copy = pltpu.make_async_copy(source, target, self.sems.at[self.used])
        self.used += 1
        copy.start()
        return copy

    def part(self, parts, masks, low, third):
        cols = slice(third * FD, (third + 1) * FD)
        copies = []
        for part, mask in zip(parts, masks):
            rows = part.shape[0]
            place = slice(None) if mask is None else rows_of(mask, rows)
            copies.append(self.start(part.at[:, cols], low.at[place, cols]))
        return copies


def wait(copies):
    for copy in copies:
        copy.wait()


def grads_kernel(masks, split, head, *refs):
    count = len(masks)
    rate_ref, key_hbm, value_hbm = refs[:3]
    parts = refs[3 : 3 + count]
    outs = refs[3 + count : -10]
    key_ref, value_ref, low, scaled, hidden, gate_grad, up_grad, update, stage, sems = refs[-10:]
    mine = slice(head * FD, (head + 1) * FD)
    copies = Copies(sems)
    key_copy = copies.start(key_hbm.at[:, mine], key_ref)
    gate_copies = copies.part(parts, masks, low, 0)
    up_copies = copies.part(parts, masks, low, 1)
    value_copy = copies.start(value_hbm.at[:, mine], value_ref)
    back_copies = copies.part(parts, masks, low, 2)
    tokens = key_ref.shape[0]
    rate = jnp.broadcast_to(rate_ref[head : head + 1, :], (8, tokens)).T[:, :1]
    block = min(256, tokens)
    for first in range(0, tokens, block):
        rows = slice(first, first + block)
        if first == 0:
            wait([key_copy] + gate_copies)
        keys = key_ref[rows, :]
        gate = dot(keys, low[:, :FD], 1, 1) * INV_ROOT
        if first == 0:
            wait(up_copies)
        up = dot(keys, low[:, FD : 2 * FD], 1, 1) * INV_ROOT
        if first == 0:
            wait([value_copy])
            scaled[...] = (rate * value_ref[...].astype(F32)).astype(BF16)
            wait(back_copies)
        back = dot(scaled[rows, :], low[:, 2 * FD :], 1, 0) * INV_ROOT
        sigmoid = 1.0 / (1.0 + jnp.exp(-gate))
        silu = gate * sigmoid
        hidden[rows, :] = (silu * up).astype(BF16)
        gate_grad[rows, :] = (back * up * sigmoid * (1.0 + gate * (1.0 - sigmoid))).astype(BF16)
        up_grad[rows, :] = (back * silu).astype(BF16)
    sent = []
    for third, (left, right) in enumerate(((gate_grad, key_ref), (up_grad, key_ref), (scaled, hidden))):
        cols = slice(third * FD, (third + 1) * FD)
        for first in range(0, FD, 128):
            rows = slice(first, first + 128)
            update[rows, cols] = dot(left[:, rows], right[...], 0, 0)
        if split:
            far, near, across, own = outs
            rows = far.shape[0]
            for number, (out, mask) in enumerate(((far, 3), (near, 1), (across, 2))):
                place = slice(number * rows, (number + 1) * rows)
                stage[place, cols] = update[rows_of(mask, rows), cols].astype(BF16)
                sent.append(copies.start(stage.at[place, cols], out.at[:, cols]))
            sent.append(copies.start(update.at[rows_of(0, rows), cols], own.at[:, cols]))
        else:
            sent.append(copies.start(update.at[:, cols], outs[0].at[:, cols]))
    wait(sent)


def head_grads(fw_key, fw_value, fw_rate, gathered, head, split):
    tokens = fw_key.shape[0]
    parts = [part for part, _ in gathered]
    masks = [mask for _, mask in gathered]
    if split:
        rows = parts[0].shape[0]
        out_shape = tuple(jax.ShapeDtypeStruct((rows, SPAN), kind) for kind in (BF16, BF16, BF16, F32))
    else:
        out_shape = (jax.ShapeDtypeStruct((FD, SPAN), F32),)
    by_token = pltpu.VMEM((tokens, FD), BF16)
    return pl.pallas_call(
        functools.partial(grads_kernel, masks, split, head),
        in_specs=[pl.BlockSpec(memory_space=pltpu.VMEM)] + [ANY] * (2 + len(parts)),
        out_specs=tuple(ANY for _ in out_shape),
        out_shape=out_shape,
        scratch_shapes=[
            by_token,
            by_token,
            pltpu.VMEM((FD, SPAN), BF16),
            by_token,
            by_token,
            by_token,
            by_token,
            pltpu.VMEM((FD, SPAN), F32),
            pltpu.VMEM((3 * parts[0].shape[0] if split else 16, SPAN), BF16),
            pltpu.SemaphoreType.DMA((2 + 3 * len(parts) + 3 * len(out_shape),)),
        ],
        compiler_params=PARAMS,
        cost_estimate=cost(12 * tokens * FD * FD, 8e6, tokens * FD),
        name="head_grads",
    )(fw_rate.T, fw_key, fw_value, *parts)


def add_kernel(left_ref, right_ref, sum_ref):
    sum_ref[...] = (left_ref[...].astype(F32) + right_ref[...].astype(F32)).astype(BF16)


def add_rows(left, right):
    rows, width = left.shape
    block = row_block(rows, 80)
    spec = pl.BlockSpec((block, width), lambda i: (i, 0))
    return pl.pallas_call(
        add_kernel,
        grid=(rows // block,),
        in_specs=[spec, spec],
        out_specs=spec,
        out_shape=jax.ShapeDtypeStruct((rows, width), BF16),
        compiler_params=PARAMS,
        cost_estimate=cost(rows * width, 6 * rows * width),
        name="add_rows",
    )(left, right)


def round_kernel(w_ref, low_ref):
    low_ref[...] = w_ref[...].astype(BF16)


def row_block(rows, most):
    return max((size for size in range(16, most + 1, 16) if rows % size == 0), default=rows)


def round_head(fast_weights, head):
    rows = fast_weights.shape[0]
    block = row_block(rows, 80)
    return pl.pallas_call(
        round_kernel,
        grid=(rows // block,),
        in_specs=[pl.BlockSpec((block, SPAN), lambda i: (i, head))],
        out_specs=pl.BlockSpec((block, SPAN), lambda i: (i, 0)),
        out_shape=jax.ShapeDtypeStruct((rows, SPAN), BF16),
        compiler_params=PARAMS,
        cost_estimate=cost(rows * SPAN, 6 * rows * SPAN),
        name="round_head",
    )(fast_weights)


def pack_kernel(q_ref, k_ref, v_ref, queries_ref, pairs_ref):
    first, width = queries_ref.shape[1], pairs_ref.shape[1] // 2
    queries_ref[...] = q_ref[...]
    pairs_ref[:, :width] = k_ref[:, first:]
    pairs_ref[:, width:] = v_ref[:, first:]


def pack_travellers(attn_query, attn_key, attn_value, stay):
    rows, width = attn_query.shape
    block = row_block(rows, 256)
    left, right = stay * HD, width - stay * HD

    def spec(cols):
        return pl.BlockSpec((block, cols), lambda i: (i, 0))

    widths = (left, 2 * right)
    return pl.pallas_call(
        pack_kernel,
        grid=(rows // block,),
        in_specs=[spec(left), spec(width), spec(width)],
        out_specs=[spec(cols) for cols in widths],
        out_shape=[jax.ShapeDtypeStruct((rows, cols), BF16) for cols in widths],
        compiler_params=PARAMS,
        cost_estimate=cost(0, 8 * rows * width),
        name="pack_travellers",
    )(attn_query, attn_key, attn_value)


def move_kernel(sums, w_ref, m_ref, *refs):
    addends = refs[:sums]
    nw_ref, nm_ref, low_ref = refs[-3:]
    update = addends[0][...]
    for addend in addends[1:]:
        update = update + addend[...].astype(F32)
    weights = w_ref[...]
    momentum = DECAY * m_ref[...] + update
    moved = weights + momentum
    nm_ref[...] = momentum
    for part in range(3):
        cols = slice(part * FD, (part + 1) * FD)
        before = jnp.mean(jnp.square(weights[:, cols]), axis=1, keepdims=True)
        after = jnp.mean(jnp.square(moved[:, cols]), axis=1, keepdims=True)
        fresh = moved[:, cols] * (jnp.sqrt(before + EPSILON) * lax.rsqrt(after + EPSILON))
        nw_ref[:, cols] = fresh
        low_ref[:, cols] = fresh.astype(BF16)


def move_weights(fast_weights, momentum, addends, head, previous):
    rows = fast_weights.shape[0]
    block = row_block(rows, 80)
    wide = pl.BlockSpec((block, SPAN), lambda i: (i, head))
    own = pl.BlockSpec((block, SPAN), lambda i: (i, 0))
    in_specs = [wide, wide] + [own] * len(addends)
    args = [fast_weights, momentum] + list(addends)
    aliases = {}
    if previous is not None:
        aliases = {len(args): 0, len(args) + 1: 1}
        in_specs += [ANY, ANY]
        args += list(previous)
    full = jax.ShapeDtypeStruct(fast_weights.shape, F32)
    return pl.pallas_call(
        functools.partial(move_kernel, len(addends)),
        grid=(rows // block,),
        in_specs=in_specs,
        out_specs=(wide, wide, own),
        out_shape=(full, full, jax.ShapeDtypeStruct((rows, SPAN), BF16)),
        input_output_aliases=aliases,
        compiler_params=PARAMS,
        cost_estimate=cost(20 * rows * SPAN, 26 * rows * SPAN),
        name="move_weights",
    )(*args)


def query_kernel(masks, q_hbm, head, *refs):
    count = len(masks)
    parts = refs[:count]
    out_hbm, q_ref, low, stage, sems = refs[-5:]
    mine = slice(head * FD, (head + 1) * FD)
    copies = Copies(sems)
    query_copy = copies.start(q_hbm.at[:, mine], q_ref)
    loads = [copies.part(parts, masks, low, third) for third in range(3)]
    tokens = q_ref.shape[0]
    block = min(256, tokens)
    sent = []
    for first in range(0, tokens, block):
        rows = slice(first, first + block)
        if first == 0:
            wait([query_copy] + loads[0])
        queries = q_ref[rows, :]
        gate = dot(queries, low[:, :FD], 1, 1) * INV_ROOT
        if first == 0:
            wait(loads[1])
        up = dot(queries, low[:, FD : 2 * FD], 1, 1) * INV_ROOT
        hidden = (gate * (1.0 / (1.0 + jnp.exp(-gate))) * up).astype(BF16)
        if first == 0:
            wait(loads[2])
        stage[rows, :] = (dot(hidden, low[:, 2 * FD :], 1, 1) * INV_ROOT).astype(BF16)
        sent.append(copies.start(stage.at[rows, :], out_hbm.at[rows, mine]))
    wait(sent)


def head_query(fw_query, gathered, head, previous):
    tokens = fw_query.shape[0]
    parts = [part for part, _ in gathered]
    masks = [mask for _, mask in gathered]
    args = [fw_query] + parts
    aliases = {}
    if previous is not None:
        aliases = {len(args): 0}
        args.append(previous)
    by_token = pltpu.VMEM((tokens, FD), BF16)
    return pl.pallas_call(
        lambda q_hbm, *refs: query_kernel(masks, q_hbm, head, *refs),
        in_specs=[ANY] * len(args),
        out_specs=ANY,
        out_shape=jax.ShapeDtypeStruct(fw_query.shape, BF16),
        scratch_shapes=[
            by_token,
            pltpu.VMEM((FD, SPAN), BF16),
            by_token,
            pltpu.SemaphoreType.DMA((1 + 3 * len(parts) + pl.cdiv(tokens, 256),)),
        ],
        input_output_aliases=aliases,
        compiler_params=PARAMS,
        cost_estimate=cost(6 * tokens * FD * FD, 4e6, tokens * FD),
        name="head_query",
    )(*args)


def swapped(array, mask):
    devices = lax.axis_size("ctx")
    return lax.ppermute(array, "ctx", [(i, i ^ mask) for i in range(devices)])


def shifted(array, by):
    devices = lax.axis_size("ctx")
    pairs = [(i, i + by) for i in range(devices) if 0 <= i + by < devices]
    return lax.ppermute(array, "ctx", pairs)


def after(array, *others):
    return lax.optimization_barrier((array,) + others)[0]


def gather_rows(shard, paired):
    if not paired:
        return [(lax.all_gather(shard, "ctx", axis=0, tiled=True), None)]
    across = swapped(shard, 2)
    beside = swapped(shard, 1)
    return [(shard, 0), (beside, 1), (across, 2), (swapped(across, 1), 3)]


def sum_rows(pieces, paired):
    if not paired:
        return [lax.psum_scatter(pieces[0], "ctx", scatter_dimension=0, tiled=True)], pieces[0]
    far, near, across, own = pieces
    far = swapped(far, 1)
    near = swapped(near, 1)
    total = add_rows(across, far)
    return [own, near, swapped(total, 2)], total


def per_device(
    attn_query, attn_key, attn_value, fw_query, fw_key, fw_value, fw_rate, fast_weights, momentum
):
    devices = lax.axis_size("ctx")
    head_local = fw_rate.shape[1]
    paired = devices == 4
    heads = range(head_local)
    all_heads = attn_query.shape[1] // HD
    moved = all_heads // 5
    stay = all_heads - moved
    half = stay // 2 if stay % 2 == 0 else stay
    halves = range(0, stay, half)

    low = round_head(fast_weights, 0)
    gathered = [gather_rows(low, paired)]
    started = gathered[0][2 if paired else 0][0]
    own = attention_call(
        own_kernel,
        stay,
        [after(attn_query, low), attn_key, attn_value],
        [0, 0, 0],
        [("t", 0), ("s", 0)],
        0.6,
        most=half,
    )
    before = own[1]
    lows = []
    for head in heads[1:]:
        low = round_head(after(fast_weights, before), head)
        before = low
        lows.append(low)
    queries, pairs = pack_travellers(after(attn_query, before), attn_key, attn_value, stay)
    for head in heads[1:]:
        gathered.append(gather_rows(after(lows[head - 1], pairs), paired))
    far_query = shifted(after(queries, started), -2)
    far_pairs = shifted(after(pairs, started), 2)
    far_pairs_other = swapped(far_pairs, 1)
    pair_key = swapped(attn_key, 1)
    pair_value = swapped(attn_value, 1)

    before = queries
    sums = []
    totals = []
    for head in heads:
        pieces = head_grads(after(fw_key, before), fw_value, fw_rate, gathered[head], head, paired)
        before = pieces[-1]
        addends, total = sum_rows(pieces, paired)
        sums.append(addends)
        totals.append(total)
    before = totals[-1]
    fw_new = None
    new_gathered = []
    found = []
    for number in range(max(len(halves), head_local)):
        if number < len(halves):
            first = halves[number]
            far_o, own_o, own_st = attention_call(
                group_kernel,
                half,
                [
                    attn_query,
                    after(far_query, before),
                    attn_key,
                    attn_value,
                    pair_key,
                    pair_value,
                    *own,
                ],
                [first] * 6 + [("t", first), ("s", first)],
                [("f", 0), ("t", 0), ("s", 0)],
                1.6,
                most=half,
            )
            found.append((far_o, own_o, own_st))
            before = own_st
        if number < head_local:
            new_weights, new_momentum, low = move_weights(
                fast_weights, after(momentum, before), sums[number], number, fw_new
            )
            fw_new = (new_weights, new_momentum)
            new_gathered.append(gather_rows(low, paired))
            before = low
    attn_out = attention_call(
        whole_kernel,
        moved,
        [
            after(attn_query, before),
            attn_key,
            attn_value,
            pair_key,
            pair_value,
            far_pairs,
            far_pairs,
            far_pairs_other,
            far_pairs_other,
        ],
        [stay] * 5 + [0, moved, 0, moved],
        [stay],
        2.2,
        (attn_query.shape, None),
        most=2,
    )[0]
    returned = []
    for number, (far_o, own_o, own_st) in enumerate(found):
        if number > 0:
            far_o = after(far_o, low)
        returned.append((own_o, own_st, shifted(far_o, 2)))
    fw_out = None
    for head in heads:
        fw_out = head_query(fw_query, new_gathered[head], head, fw_out)
    for number, states in enumerate(returned):
        attn_out = attention_call(
            merge_kernel,
            half,
            states,
            [("t", 0), ("s", 0), ("f", 0)],
            [number * half],
            0.01,
            (attn_query.shape, attn_out),
            most=half,
        )[0]
    return (attn_out, fw_out, new_weights, new_momentum)


def solution(mesh):
    spec = P(("seq", "ctx"), "head")

    return jax.shard_map(
        per_device, mesh=mesh, in_specs=(spec,) * 9, out_specs=(spec,) * 4, check_vma=False
    )
```
